32 devices in a mesh: groups: 2 (over y), bins: 4 (over z), fdot: 4 (over x, core).
Axes of the slice: x: 2, y: 2, z: 4, core: 2. Of those that a mesh axis runs over, the one named last changes fastest.
Arguments:
- spectrum: float32 [2, 262144], P(None, ('groups', 'bins')), parts along dimension 1, may hold values from -80 to 80
- bank: bfloat16 [128, 2, 128], replicated, may hold values from -0.5 to 0.5
- fdot_index: int32 [32], P('fdot'), may hold values from 0 to 127
- harm_map: int32 [7, 4, 4], P(None, 'bins'), may hold values from 0 to 28672, as said below
Outputs:
- harmonic_power: float32 [32, 262144], P('fdot', ('groups', 'bins')), parts along dimension 1
The draws below stay inside these ranges and needn't reach their ends.
There are 2 independent parts, one for each index of `groups`. The reference program is written for one: setup_inputs(seed, part) draws one part's arguments, and reference() takes and returns one part's arrays. A program takes and returns all parts, laid end to end along the dimension named above; an argument that names none is the same for every part. Nothing has to cross between parts.
Inputs may be any that keep to these rules, and one draw needn't show every extreme that they name: harm_map[q, d] = (floor(d s / 8), s, (d * 32768 s / 8) mod 32768, p) with s = 4, 2, 6, 1, 3, 5, 7 for q = 0 .. 6 and a rounding phase p in 0 .. 7.
All inputs are finite; a program needn't handle non-finite values.
Results may differ from the reference program's by a relative error of at most 0.0003.
The reference program's roundings to bfloat16 on the way (of `normed` and `kernels`) count: a program that leaves them out, or rounds other values in their place, can miss the bound.
Values may be sent and summed in bfloat16 or wider, within the bound.
A program may use at most 64 MiB of HBM per device.

```python
import math
import jax
import jax.numpy as jnp
from jax import lax

BLK = 32768
ZT = 32
W = 128
NBANK = 128
NFRAC = 7
BINS = 131072
NBLK = 4
N_BINS = 4


def draw_spectrum(key, part):
    key_scale = jax.random.fold_in(key, 11)
    key_base = jax.random.fold_in(key, 12)
    index = jnp.arange(BINS, dtype=jnp.float32)
    rough = jnp.exp(jax.random.uniform(key_scale, (BINS,), jnp.float32, math.log(0.3), math.log(3.0)))
    envelope = jnp.sqrt(1.0 + 2.0 * index / BINS)
    base = jnp.clip(jax.random.normal(key_base, (2, BINS), jnp.float32), -5.0, 5.0)
    target = base * (rough * envelope)[None, :]
    partner = jnp.concatenate([target[:, :1], target[:, :0:-1]], axis=1)
    even_real = 0.5 * (target[0] + partner[0])
    even_imag = 0.5 * (target[1] - partner[1])
    diff_real = 0.5 * (target[0] - partner[0])
    diff_imag = 0.5 * (target[1] + partner[1])
    angle = index * (math.pi / BINS)
    cosine = jnp.cos(angle)
    sine = jnp.sin(angle)
    odd_real = diff_real * cosine - diff_imag * sine
    odd_imag = diff_real * sine + diff_imag * cosine
    return jnp.stack([even_real - odd_imag, even_imag + odd_real]).astype(jnp.float32)


def draw_harm_map(key, part):
    numerators = jnp.array([4, 2, 6, 1, 3, 5, 7], jnp.int32)[:, None]
    blocks = jnp.arange(NBLK, dtype=jnp.int32)[None, :]
    source = jnp.broadcast_to(blocks * numerators // 8, (NFRAC, NBLK))
    stride = jnp.broadcast_to(numerators, (NFRAC, NBLK))
    offset = jnp.broadcast_to(blocks * numerators % 8 * (BLK // 8), (NFRAC, NBLK))
    phase = jax.random.randint(jax.random.fold_in(key, 21), (NFRAC, NBLK), 0, 8, dtype=jnp.int32)
    return jnp.stack([source, stride, offset, phase], axis=-1).astype(jnp.int32)


def with_ends(values, rng, least, high):
    extent = values.shape
    spot = [jax.random.randint(jax.random.fold_in(rng, axis), (), 0, extent[axis]) for axis in range(len(extent))]
    values = values.at[tuple(spot)].set(least)
    longest = extent.index(max(extent))
    spot[longest] = (spot[longest] + 1) % extent[longest]
    return values.at[tuple(spot)].set(high)


def scatter_about(own_key, shape, width, most, kind=jnp.bfloat16):
    drawn = jax.random.normal(own_key, shape, jnp.float32) * width
    return jnp.minimum(jnp.maximum(drawn, -most), most).astype(kind)


def setup_inputs(seed: int = 0, part: int = 0) -> dict:
    seeds = jax.random.split(jax.random.key(seed), 5)
    part_splits = jax.random.split(jax.random.fold_in(seeds[4], part), 5)
    spectrum = draw_spectrum(jax.random.fold_in(jax.random.fold_in(seeds[4], part), 71), part)
    bank = scatter_about(seeds[1], (NBANK, 2, W), W ** -0.5, 0.5)
    fdot_index = with_ends(jax.random.randint(seeds[2], (ZT,), 0, NBANK), jax.random.fold_in(seeds[2], 1), 0, NBANK - 1).astype(jnp.int32)
    harm_map = draw_harm_map(jax.random.fold_in(seeds[4], 71), part)
    return {"spectrum": spectrum, "bank": bank, "fdot_index": fdot_index, "harm_map": harm_map}


def unpack(packed, mirrored, positions, total_bins):
    real_a, imag_a = (packed[0], packed[1])
    real_b, imag_b = (mirrored[0], mirrored[1])
    even_real = 0.5 * (real_a + real_b)
    even_imag = 0.5 * (imag_a - imag_b)
    odd_real = 0.5 * (imag_a + imag_b)
    odd_imag = 0.5 * (real_b - real_a)
    angle = positions.astype(jnp.float32) * jnp.float32(math.pi / total_bins)
    cosine = jnp.cos(angle)
    sine = jnp.sin(angle)
    out_real = even_real + cosine * odd_real + sine * odd_imag
    out_imag = even_imag + cosine * odd_imag - sine * odd_real
    return (out_real, out_imag)

def toeplitz(kernel):
    row_count = kernel.shape[0]
    length = kernel.shape[1]
    padded = jnp.concatenate([kernel, jnp.zeros((row_count, length + 1), kernel.dtype)], axis=1)
    repeated = jnp.tile(padded, (1, length))[:, :2 * length * length]
    return repeated.reshape(row_count, length, 2 * length)

def template_weights(bank, fdot_index, kernel_len):
    n_bank = bank.shape[0]
    onehot = (fdot_index[:, None] == jnp.arange(n_bank, dtype=jnp.int32)[None, :]).astype(jnp.bfloat16)
    kernels = jnp.dot(onehot, bank.reshape(n_bank, 2 * kernel_len), preferred_element_type=jnp.float32).astype(jnp.bfloat16)
    real_part = toeplitz(kernels[:, :kernel_len])
    imag_part = toeplitz(kernels[:, kernel_len:])
    return jnp.stack([jnp.concatenate([real_part, -imag_part], axis=2), jnp.concatenate([imag_part, real_part], axis=2)])

def correlate(padded, weights, kernel_len):
    length = padded.shape[1] - kernel_len
    count = length // kernel_len
    lower = padded[:, :length].reshape(2, count, kernel_len)
    upper = padded[:, kernel_len:].reshape(2, count, kernel_len)
    stacked = jnp.concatenate([lower[0], upper[0], lower[1], upper[1]], axis=1)
    amps = jnp.einsum('ta,krca->krtc', stacked.astype(jnp.float32), weights.astype(jnp.float32))
    return (amps[0] * amps[0] + amps[1] * amps[1]).reshape(weights.shape[1], length)

def reference(spectrum, bank, fdot_index, harm_map):
    total_bins = BLK * N_BINS
    mirrored = jnp.concatenate([spectrum[:, :1], spectrum[:, :0:-1]], axis=1)
    positions = jnp.arange(total_bins, dtype=jnp.int32)
    out_real, out_imag = unpack(spectrum, mirrored, positions, total_bins)
    total_power = jnp.sum(out_real * out_real + out_imag * out_imag)
    scaling = lax.rsqrt(total_power / total_bins + 1e-06)
    normed = jnp.stack([out_real * scaling, out_imag * scaling]).astype(jnp.bfloat16)
    weights = template_weights(bank, fdot_index, W)
    half = W // 2
    padded = jnp.pad(normed, ((0, 0), (half, half)))

    def block_plane(start):
        window = lax.dynamic_slice(padded, (jnp.int32(0), start.astype(jnp.int32)), (2, BLK + W))
        return correlate(window, weights, W)
    planes = lax.map(block_plane, jnp.arange(N_BINS, dtype=jnp.int32) * BLK)
    plane = planes.transpose(1, 0, 2).reshape(ZT, total_bins)
    total = plane
    offsets = jnp.arange(BLK, dtype=jnp.int32)
    for fraction in range(NFRAC):
        entry = harm_map[fraction].astype(jnp.int32)
        source = entry[:, 0:1] * BLK + entry[:, 2:3] + (offsets[None, :] * entry[:, 1:2] + entry[:, 3:4]) // 8
        total = total + jnp.take(plane, source.reshape(-1), axis=1)
    return total * 0.125
```

```python
import math

import jax
import jax.numpy as jnp
from jax import lax
from jax.experimental import pallas as pl
from jax.experimental.pallas import tpu as pltpu
from jax.sharding import PartitionSpec as P

LANES = 128
STRIDE_TABLE = (4, 2, 6, 1, 3, 5, 7)


def from_behind(value, axis, steps):
    count = lax.axis_size(axis)
    pairs = [(source, (source + steps) % count) for source in range(count)]
    return lax.ppermute(value, axis, pairs)


def from_partner(value, axis, apart):
    mask = 2**apart
    pairs = [(source, source ^ mask) for source in range(lax.axis_size(axis))]
    return lax.ppermute(value, axis, pairs)


def unpack(packed, mirrored, positions, total_bins):
    real_a, imag_a = (packed[0], packed[1])
    real_b, imag_b = (mirrored[0], mirrored[1])
    even_real = 0.5 * (real_a + real_b)
    even_imag = 0.5 * (imag_a - imag_b)
    odd_real = 0.5 * (imag_a + imag_b)
    odd_imag = 0.5 * (real_b - real_a)
    angle = positions.astype(jnp.float32) * jnp.float32(math.pi / total_bins)
    cosine = jnp.cos(angle)
    sine = jnp.sin(angle)
    out_real = even_real + cosine * odd_real + sine * odd_imag
    out_imag = even_imag + cosine * odd_imag - sine * odd_real
    return (out_real, out_imag)


def search_layout(block_rows):
    spans = [(8, 0, block_rows)]
    row = block_rows
    for stride in STRIDE_TABLE:
        count = stride * block_rows // 8 + 16
        spans.append((stride, row, count))
        row += count
    return spans, -(-row // 256) * 256


def search_kernel(block_rows, templates, harm_ref, index_ref, bank_ref, spec_ref, out_ref,
                  lines_ref, window_ref, weight_ref, plane_ref):
    spans, window_rows = search_layout(block_rows)
    total_rows = spec_ref.shape[1]
    position = lax.axis_index("bins")
    n_bank = bank_ref.shape[0]
    lane_of = lax.broadcasted_iota(jnp.int32, (templates, n_bank), 1)
    onehot = jnp.where(index_ref[...] == lane_of, 1.0, 0.0).astype(jnp.bfloat16)
    taps = jnp.dot(onehot, bank_ref[...], preferred_element_type=jnp.float32).astype(jnp.bfloat16)
    tap = lax.broadcasted_iota(jnp.int32, (LANES, 2 * LANES), 0)
    lane = lax.broadcasted_iota(jnp.int32, (LANES, 2 * LANES), 1)
    turn = jnp.where((tap + lane) % (2 * LANES) == 0, 1.0, 0.0).astype(jnp.bfloat16)
    turned = [
        jnp.dot(taps[:, part * LANES : (part + 1) * LANES], turn, preferred_element_type=jnp.float32)
        for part in range(2)
    ]
    for template in range(templates):
        parts = []
        for part in range(2):
            row = jnp.broadcast_to(turned[part][template : template + 1, :], (2 * LANES, 2 * LANES))
            rolled = pltpu.roll(row, 0, 1, stride=1, stride_axis=0)
            parts.append(rolled[:, :LANES].astype(jnp.bfloat16))
        real, imag = parts
        weight_ref[template, : 2 * LANES, :LANES] = real
        weight_ref[template, : 2 * LANES, LANES:] = imag
        weight_ref[template, 2 * LANES :, :LANES] = -imag
        weight_ref[template, 2 * LANES :, LANES:] = real
    low_half = lax.broadcasted_iota(jnp.int32, (1, LANES), 1) < LANES // 2
    for part in range(2):
        lines_ref[part, :8, :] = jnp.zeros((8, LANES), jnp.float32)
        lines_ref[part, pl.ds(8 + total_rows, 8), :] = jnp.zeros((8, LANES), jnp.float32)

        @pl.loop(0, total_rows // 256)
        def _(step, part=part):
            row = pl.multiple_of(step * 256, 256)
            lines_ref[part, pl.ds(row + 8, 256), :] = spec_ref[part, pl.ds(row, 256), :].astype(
                jnp.float32
            )

    for stride, first, count in spans:
        start = position * (stride * block_rows // 8)
        piece = 16
        for part in range(2):

            @pl.loop(0, count // piece)
            def _(step, part=part, first=first, start=start):
                row = pl.multiple_of(step * piece, piece)
                source = pl.multiple_of(start + row, 8)
                before = pltpu.roll(lines_ref[part, pl.ds(source + 7, piece), :], LANES // 2, 1)
                here = pltpu.roll(lines_ref[part, pl.ds(source + 8, piece), :], LANES // 2, 1)
                after = pltpu.roll(lines_ref[part, pl.ds(source + 9, piece), :], LANES // 2, 1)
                target = pl.ds(pl.multiple_of(first + row, piece), piece)
                window_ref[target, pl.ds(2 * part * LANES, LANES)] = jnp.where(
                    low_half, before, here
                ).astype(jnp.bfloat16)
                window_ref[target, pl.ds((2 * part + 1) * LANES, LANES)] = jnp.where(
                    low_half, here, after
                ).astype(jnp.bfloat16)

    used = spans[-1][1] + spans[-1][2]
    if used < window_rows:
        window_ref[used:, :] = jnp.zeros((window_rows - used, 4 * LANES), jnp.bfloat16)

    @pl.loop(0, window_rows // 256)
    def _(step):
        row = pl.multiple_of(step * 256, 256)
        lhs = window_ref[pl.ds(row, 256), :]
        for template in range(templates):
            amps = jnp.dot(lhs, weight_ref[template], preferred_element_type=jnp.float32)
            real, imag = amps[:, :LANES], amps[:, LANES:]
            plane_ref[pl.ds(row * templates + template, 256, stride=templates), :] = (
                real * real + imag * imag
            )

    column = lax.broadcasted_iota(jnp.int32, (templates, LANES), 1)

    @pl.loop(0, block_rows // 8)
    def _(group):
        sums = []
        for unit in range(8):
            row = pl.multiple_of((group * 8 + unit) * templates, templates)
            sums.append(plane_ref[pl.ds(row, templates), :])
        for number, (stride, first, _) in enumerate(spans[1:]):
            base = (column * stride + harm_ref[number, 3]) // 8

            def source_row(line, first=first, stride=stride):
                row = (first + group * stride + line) * templates
                return plane_ref[pl.ds(pl.multiple_of(row, templates), templates), :]

            for unit in range(8):
                begin = unit * stride * (LANES // 8)
                line, offset = begin // LANES, begin % LANES
                where = base + offset
                wrapped = where & (LANES - 1)
                picked = jnp.take_along_axis(source_row(line), wrapped, axis=1)
                if offset + stride * (LANES // 8) >= LANES:
                    follow = jnp.take_along_axis(source_row(line + 1), wrapped, axis=1)
                    picked = jnp.where(where < LANES, picked, follow)
                sums[unit] = sums[unit] + picked
        for unit in range(8):
            row = pl.multiple_of((group * 8 + unit) * templates, templates)
            out_ref[pl.ds(row, templates), :] = sums[unit] * 0.125


def search(normed_rows, bank, fdot_index, harm_map, block_rows):
    own = fdot_index.shape[0]
    templates = -(-own // 8) * 8
    n_bank = bank.shape[0]
    total_rows = normed_rows.shape[1]
    spans, window_rows = search_layout(block_rows)
    index = jnp.pad(fdot_index, (0, templates - own)).reshape(templates, 1)
    vmem = pl.BlockSpec(memory_space=pltpu.VMEM)

    def kernel(*refs):
        search_kernel(block_rows, templates, *refs)

    out = pl.pallas_call(
        kernel,
        out_shape=jax.ShapeDtypeStruct((block_rows * templates, LANES), jnp.float32),
        in_specs=[pl.BlockSpec(memory_space=pltpu.SMEM), vmem, vmem, vmem],
        out_specs=vmem,
        scratch_shapes=[
            pltpu.VMEM((2, total_rows + 16, LANES), jnp.float32),
            pltpu.VMEM((window_rows, 4 * LANES), jnp.bfloat16),
            pltpu.VMEM((templates, 4 * LANES, 2 * LANES), jnp.bfloat16),
            pltpu.VMEM((window_rows * templates, LANES), jnp.float32),
        ],
        compiler_params=pltpu.CompilerParams(vmem_limit_bytes=56 * 1024 * 1024),
        name="search",
    )(harm_map[:, 0, :], index, bank.reshape(n_bank, 2 * LANES), normed_rows)
    out = out.reshape(block_rows, templates, LANES).transpose(1, 0, 2)
    return out.reshape(templates, block_rows * LANES)[:own]


def body(spectrum, bank, fdot_index, harm_map):
    block_len = spectrum.shape[1]
    bin_devices = lax.axis_size("bins")
    position = lax.axis_index("bins")
    total_bins = block_len * bin_devices
    first_bin = spectrum[:, :1]
    next_first = from_behind(first_bin, "bins", -1)
    partner, partner_first = (spectrum, next_first)
    for bit_number in range(bin_devices.bit_length() - 1):
        partner, partner_first = from_partner((partner, partner_first), "bins", bit_number)
    mirrored = jnp.concatenate([partner_first, partner[:, :0:-1]], axis=1)
    positions = position * block_len + jnp.arange(block_len, dtype=jnp.int32)
    out_real, out_imag = unpack(spectrum, mirrored, positions, total_bins)
    local_power = jnp.sum(out_real * out_real + out_imag * out_imag)
    total_power = lax.psum(local_power, "bins")
    scaling = lax.rsqrt(total_power / total_bins + 1e-06)
    normed = jnp.stack([out_real * scaling, out_imag * scaling]).astype(jnp.bfloat16)
    whole_spectrum = lax.all_gather(normed, "bins", axis=1, tiled=True)
    rows = whole_spectrum.reshape(2, total_bins // LANES, LANES)
    return search(rows, bank, fdot_index, harm_map, block_len // LANES)


def solution(mesh):
    placed = (P(None, ("groups", "bins")), P(), P("fdot"), P(None, "bins", None))
    return jax.shard_map(
        body, mesh=mesh, in_specs=placed, out_specs=P("fdot", ("groups", "bins")), check_vma=False
    )
```

```python
import math

import jax
import jax.numpy as jnp
from jax import lax
from jax.experimental import pallas as pl
from jax.experimental.pallas import tpu as pltpu
from jax.sharding import PartitionSpec as P

LANES = 128
STRIDE_TABLE = (4, 2, 6, 1, 3, 5, 7)


def spread_kernel(bins, spec_ref, out_ref, mirror_ref, tiles_ref, trade_send, trade_recv,
                  tile_send, tile_recv, part_send, part_recv, mate_send, mate_recv):
    mesh_ids = pl.DeviceIdType.MESH
    block_rows = spec_ref.shape[0] // 2
    half = block_rows // 2
    place = lax.axis_index("bins")
    member = lax.axis_index("fdot")
    side = lax.rem(member, 2)
    mate = member + 1 - 2 * side
    partner = bins - 1 - place
    total_bins = bins * block_rows * LANES
    lane = lax.broadcasted_iota(jnp.int32, (half, LANES), 1)
    line = lax.broadcasted_iota(jnp.int32, (half, LANES), 0)

    power = jnp.zeros((8, LANES), jnp.float32)
    for first in range(0, 2 * block_rows, 64):
        chunk = spec_ref[first : first + 64, :]
        square = chunk * chunk
        if first == 0:
            row8 = lax.broadcasted_iota(jnp.int32, (64, LANES), 0)
            lane8 = lax.broadcasted_iota(jnp.int32, (64, LANES), 1)
            both = chunk[0:1, :] + chunk[1:2, :]
            is_first = (lane8 == 0) & (place == 0)
            square = jnp.where(is_first & (row8 == 0), both * both, square)
            square = jnp.where(is_first & (row8 == 1), 0.0, square)
        power = power + jnp.sum(square.reshape(8, 8, LANES), axis=0)
    tiles_ref[place, :8, :] = power
    tiles_ref[place, 8:, :] = spec_ref[:8, :]
    mirror_ref[2 * half + 8 :, :] = jnp.zeros((8, LANES), jnp.float32)

    barrier = pltpu.get_barrier_semaphore()
    for step in range(1, bins):
        pl.semaphore_signal(
            barrier, inc=1, device_id={"bins": lax.rem(place + step, bins)}, device_id_type=mesh_ids
        )
    pl.semaphore_signal(barrier, inc=1, device_id={"fdot": mate}, device_id_type=mesh_ids)
    pl.semaphore_wait(barrier, bins)

    start = pl.multiple_of((1 - side) * (2 * half - 8), 8)
    trade = pltpu.make_async_remote_copy(
        src_ref=spec_ref.at[pl.ds(start, 2 * half + 8), :],
        dst_ref=mirror_ref.at[pl.ds(0, 2 * half + 8), :],
        send_sem=trade_send,
        recv_sem=trade_recv,
        device_id={"bins": partner},
        device_id_type=mesh_ids,
    )
    tile_copies = []
    for step in range(1, bins):
        tile_copies.append(
            pltpu.make_async_remote_copy(
                src_ref=tiles_ref.at[place],
                dst_ref=tiles_ref.at[place],
                send_sem=tile_send.at[step],
                recv_sem=tile_recv.at[step],
                device_id={"bins": lax.rem(place + step, bins)},
                device_id_type=mesh_ids,
            )
        )
    for copy in tile_copies:
        copy.start()
    trade.start()

    position = place * (block_rows * LANES) + (side * half + line) * LANES + lane
    angle = position.astype(jnp.float32) * jnp.float32(math.pi / total_bins)
    cosine = jnp.cos(angle)
    sine = jnp.sin(angle)

    for step in range(1, bins):
        source = lax.rem(place + bins - step, bins)
        pltpu.make_async_remote_copy(
            src_ref=tiles_ref.at[source],
            dst_ref=tiles_ref.at[source],
            send_sem=tile_send.at[step],
            recv_sem=tile_recv.at[step],
            device_id={"bins": lax.rem(place + step, bins)},
            device_id_type=mesh_ids,
        ).wait_recv()
    power = tiles_ref[0, :8, :]
    for other in range(1, bins):
        power = power + tiles_ref[other, :8, :]
    total = jnp.sum(jnp.sum(power, axis=0, keepdims=True), axis=1, keepdims=True)
    scaling = lax.rsqrt(total / total_bins + 1e-06)
    after = tiles_ref[lax.rem(bins - place, bins), 8:, :]

    trade.wait_recv()
    own = pl.multiple_of(side * 2 * half, 8)
    base = pl.multiple_of((1 - side) * 8, 8)
    turn = (LANES - lane[:8]) & (LANES - 1)
    flip = 7 - line[:8]
    at_last = (line == half - 1) & (side == 0)
    mirrored = []
    for part in range(2):
        here = mirror_ref[pl.ds(base + part, half, stride=2), :]
        follow = mirror_ref[pl.ds(base + part + 2, half, stride=2), :]
        follow = jnp.where(at_last, after[part : part + 1, :], follow)
        groups = []
        for first in range(half - 8, -1, -8):
            piece = jnp.take_along_axis(here[first : first + 8, :], turn, axis=1)
            piece = jnp.where(lane[:8] == 0, follow[first : first + 8, :], piece)
            groups.append(jnp.take_along_axis(piece, flip, axis=0))
        mirrored.append(jnp.concatenate(groups, axis=0))
    real_a = spec_ref[pl.ds(own, half, stride=2), :]
    imag_a = spec_ref[pl.ds(own + 1, half, stride=2), :]
    real_b, imag_b = mirrored
    even_real = 0.5 * (real_a + real_b)
    even_imag = 0.5 * (imag_a - imag_b)
    odd_real = 0.5 * (imag_a + imag_b)
    odd_imag = 0.5 * (real_b - real_a)
    out_real = even_real + cosine * odd_real + sine * odd_imag
    out_imag = even_imag + cosine * odd_imag - sine * odd_real
    mine = place * 2 + side
    out_ref[mine, 0] = (out_real * scaling).astype(jnp.bfloat16)
    out_ref[mine, 1] = (out_imag * scaling).astype(jnp.bfloat16)

    def to_bins(slot, step):
        return pltpu.make_async_remote_copy(
            src_ref=out_ref.at[slot],
            dst_ref=out_ref.at[slot],
            send_sem=part_send.at[step],
            recv_sem=part_recv.at[step],
            device_id={"bins": lax.rem(place + step, bins)},
            device_id_type=mesh_ids,
        )

    def to_mate(slot, step):
        return pltpu.make_async_remote_copy(
            src_ref=out_ref.at[slot],
            dst_ref=out_ref.at[slot],
            send_sem=mate_send.at[step],
            recv_sem=mate_recv.at[step],
            device_id={"fdot": mate},
            device_id_type=mesh_ids,
        )

    sends = [to_bins(mine, step) for step in range(1, bins)] + [to_mate(mine, 0)]
    for copy in sends:
        copy.start()
    for step in range(1, bins):
        slot = lax.rem(place + bins - step, bins) * 2 + side
        to_bins(slot, step).wait_recv()
        copy = to_mate(slot, step)
        copy.start()
        sends.append(copy)
    for step in range(bins):
        slot = lax.rem(place + bins - step, bins) * 2 + 1 - side
        to_mate(slot, step).wait_recv()
    trade.wait_send()
    for copy in tile_copies + sends:
        copy.wait_send()


def spread(spectrum):
    bins = lax.axis_size("bins")
    block_rows = spectrum.shape[1] // LANES
    half = block_rows // 2
    lines = spectrum.reshape(2, block_rows, LANES).transpose(1, 0, 2).reshape(2 * block_rows, LANES)
    vmem = pl.BlockSpec(memory_space=pltpu.VMEM)

    def kernel(*refs):
        spread_kernel(bins, *refs)

    dma = pltpu.SemaphoreType.DMA
    return pl.pallas_call(
        kernel,
        out_shape=jax.ShapeDtypeStruct((2 * bins, 2, half, LANES), jnp.bfloat16),
        in_specs=[vmem],
        out_specs=vmem,
        scratch_shapes=[
            pltpu.VMEM((2 * half + 16, LANES), jnp.float32),
            pltpu.VMEM((bins, 16, LANES), jnp.float32),
            dma, dma, dma((bins,)), dma((bins,)), dma((bins,)), dma((bins,)), dma((bins,)), dma((bins,)),
        ],
        compiler_params=pltpu.CompilerParams(collective_id=0, has_side_effects=True),
        name="spread",
    )(lines)


def search_layout(block_rows):
    spans = [(8, 0, block_rows)]
    row = block_rows
    for stride in STRIDE_TABLE:
        count = stride * block_rows // 8 + 16
        spans.append((stride, row, count))
        row += count
    return spans, -(-row // 256) * 256


def search_kernel(block_rows, templates, harm_ref, index_ref, bank_ref, spec_ref, out_ref,
                  lines_ref, window_ref, weight_ref, plane_ref):
    spans, window_rows = search_layout(block_rows)
    half = spec_ref.shape[2]
    total_rows = spec_ref.shape[0] * half
    position = lax.axis_index("bins")
    n_bank = bank_ref.shape[0]
    lane_of = lax.broadcasted_iota(jnp.int32, (templates, n_bank), 1)
    onehot = jnp.where(index_ref[...] == lane_of, 1.0, 0.0).astype(jnp.bfloat16)
    taps = jnp.dot(onehot, bank_ref[...], preferred_element_type=jnp.float32).astype(jnp.bfloat16)
    tap = lax.broadcasted_iota(jnp.int32, (LANES, 2 * LANES), 0)
    lane = lax.broadcasted_iota(jnp.int32, (LANES, 2 * LANES), 1)
    turn = jnp.where((tap + lane) % (2 * LANES) == 0, 1.0, 0.0).astype(jnp.bfloat16)
    turned = [
        jnp.dot(taps[:, part * LANES : (part + 1) * LANES], turn, preferred_element_type=jnp.float32)
        for part in range(2)
    ]
    for template in range(templates):
        parts = []
        for part in range(2):
            row = jnp.broadcast_to(turned[part][template : template + 1, :], (2 * LANES, 2 * LANES))
            rolled = pltpu.roll(row, 0, 1, stride=1, stride_axis=0)
            parts.append(rolled[:, :LANES].astype(jnp.bfloat16))
        real, imag = parts
        weight_ref[template, : 2 * LANES, :LANES] = real
        weight_ref[template, : 2 * LANES, LANES:] = imag
        weight_ref[template, 2 * LANES :, :LANES] = -imag
        weight_ref[template, 2 * LANES :, LANES:] = real
    low_half = lax.broadcasted_iota(jnp.int32, (1, LANES), 1) < LANES // 2
    for part in range(2):
        lines_ref[part, :8, :] = jnp.zeros((8, LANES), jnp.float32)
        lines_ref[part, pl.ds(8 + total_rows, 8), :] = jnp.zeros((8, LANES), jnp.float32)

        @pl.loop(0, spec_ref.shape[0])
        def _(step, part=part):
            row = pl.multiple_of(step * half, half)
            lines_ref[part, pl.ds(row + 8, half), :] = spec_ref[step, part].astype(jnp.float32)

    for stride, first, count in spans:
        start = position * (stride * block_rows // 8)
        piece = 16
        for part in range(2):

            @pl.loop(0, count // piece)
            def _(step, part=part, first=first, start=start):
                row = pl.multiple_of(step * piece, piece)
                source = pl.multiple_of(start + row, 8)
                before = pltpu.roll(lines_ref[part, pl.ds(source + 7, piece), :], LANES // 2, 1)
                here = pltpu.roll(lines_ref[part, pl.ds(source + 8, piece), :], LANES // 2, 1)
                after = pltpu.roll(lines_ref[part, pl.ds(source + 9, piece), :], LANES // 2, 1)
                target = pl.ds(pl.multiple_of(first + row, piece), piece)
                window_ref[target, pl.ds(2 * part * LANES, LANES)] = jnp.where(
                    low_half, before, here
                ).astype(jnp.bfloat16)
                window_ref[target, pl.ds((2 * part + 1) * LANES, LANES)] = jnp.where(
                    low_half, here, after
                ).astype(jnp.bfloat16)

    used = spans[-1][1] + spans[-1][2]
    if used < window_rows:
        window_ref[used:, :] = jnp.zeros((window_rows - used, 4 * LANES), jnp.bfloat16)

    @pl.loop(0, window_rows // 256)
    def _(step):
        row = pl.multiple_of(step * 256, 256)
        lhs = window_ref[pl.ds(row, 256), :]
        for template in range(templates):
            amps = jnp.dot(lhs, weight_ref[template], preferred_element_type=jnp.float32)
            real, imag = amps[:, :LANES], amps[:, LANES:]
            plane_ref[pl.ds(row * templates + template, 256, stride=templates), :] = (
                real * real + imag * imag
            )

    column = lax.broadcasted_iota(jnp.int32, (templates, LANES), 1)

    @pl.loop(0, block_rows // 8)
    def _(group):
        sums = []
        for unit in range(8):
            row = pl.multiple_of((group * 8 + unit) * templates, templates)
            sums.append(plane_ref[pl.ds(row, templates), :])
        for number, (stride, first, _) in enumerate(spans[1:]):
            base = (column * stride + harm_ref[number, 3]) // 8

            def source_row(line, first=first, stride=stride):
                row = (first + group * stride + line) * templates
                return plane_ref[pl.ds(pl.multiple_of(row, templates), templates), :]

            for unit in range(8):
                begin = unit * stride * (LANES // 8)
                line, offset = begin // LANES, begin % LANES
                where = base + offset
                wrapped = where & (LANES - 1)
                picked = jnp.take_along_axis(source_row(line), wrapped, axis=1)
                if offset + stride * (LANES // 8) >= LANES:
                    follow = jnp.take_along_axis(source_row(line + 1), wrapped, axis=1)
                    picked = jnp.where(where < LANES, picked, follow)
                sums[unit] = sums[unit] + picked
        for unit in range(8):
            row = pl.multiple_of((group * 8 + unit) * templates, templates)
            out_ref[pl.ds(row, templates), :] = sums[unit] * 0.125


def search(pieces, bank, fdot_index, harm_map, block_rows):
    own = fdot_index.shape[0]
    templates = -(-own // 8) * 8
    n_bank = bank.shape[0]
    total_rows = pieces.shape[0] * pieces.shape[2]
    spans, window_rows = search_layout(block_rows)
    index = jnp.pad(fdot_index, (0, templates - own)).reshape(templates, 1)
    vmem = pl.BlockSpec(memory_space=pltpu.VMEM)

    def kernel(*refs):
        search_kernel(block_rows, templates, *refs)

    out = pl.pallas_call(
        kernel,
        out_shape=jax.ShapeDtypeStruct((block_rows * templates, LANES), jnp.float32),
        in_specs=[pl.BlockSpec(memory_space=pltpu.SMEM), vmem, vmem, vmem],
        out_specs=vmem,
        scratch_shapes=[
            pltpu.VMEM((2, total_rows + 16, LANES), jnp.float32),
            pltpu.VMEM((window_rows, 4 * LANES), jnp.bfloat16),
            pltpu.VMEM((templates, 4 * LANES, 2 * LANES), jnp.bfloat16),
            pltpu.VMEM((window_rows * templates, LANES), jnp.float32),
        ],
        compiler_params=pltpu.CompilerParams(vmem_limit_bytes=56 * 1024 * 1024),
        name="search",
    )(harm_map[:, 0, :], index, bank.reshape(n_bank, 2 * LANES), pieces)
    out = out.reshape(block_rows, templates, LANES).transpose(1, 0, 2)
    return out.reshape(templates, block_rows * LANES)[:own]


def body(spectrum, bank, fdot_index, harm_map):
    pieces = spread(spectrum)
    return search(pieces, bank, fdot_index, harm_map, spectrum.shape[1] // LANES)


def solution(mesh):
    placed = (P(None, ("groups", "bins")), P(), P("fdot"), P(None, "bins", None))
    return jax.shard_map(
        body, mesh=mesh, in_specs=placed, out_specs=P("fdot", ("groups", "bins")), check_vma=False
    )
```

```python
import math

import jax
import jax.numpy as jnp
from jax import lax
from jax.experimental import pallas as pl
from jax.experimental.pallas import tpu as pltpu
from jax.sharding import PartitionSpec as P

LANES = 128
STRIDE_TABLE = (4, 2, 6, 1, 3, 5, 7)


def spread_kernel(bins, spec_ref, out_ref, mirror_ref, tiles_ref, trade_send, trade_recv,
                  tile_send, tile_recv, part_send, part_recv, mate_send, mate_recv):
    mesh_ids = pl.DeviceIdType.MESH
    block_rows = spec_ref.shape[0] // 2
    half = block_rows // 2
    place = lax.axis_index("bins")
    member = lax.axis_index("fdot")
    side = lax.rem(member, 2)
    mate = member + 1 - 2 * side
    partner = bins - 1 - place
    total_bins = bins * block_rows * LANES
    lane = lax.broadcasted_iota(jnp.int32, (half, LANES), 1)
    line = lax.broadcasted_iota(jnp.int32, (half, LANES), 0)

    power = jnp.zeros((8, LANES), jnp.float32)
    for first in range(0, 2 * block_rows, 64):
        chunk = spec_ref[first : first + 64, :]
        square = chunk * chunk
        if first == 0:
            row8 = lax.broadcasted_iota(jnp.int32, (64, LANES), 0)
            lane8 = lax.broadcasted_iota(jnp.int32, (64, LANES), 1)
            both = chunk[0:1, :] + chunk[1:2, :]
            is_first = (lane8 == 0) & (place == 0)
            square = jnp.where(is_first & (row8 == 0), both * both, square)
            square = jnp.where(is_first & (row8 == 1), 0.0, square)
        power = power + jnp.sum(square.reshape(8, 8, LANES), axis=0)
    tiles_ref[place, :8, :] = power
    tiles_ref[place, 8:, :] = spec_ref[:8, :]
    mirror_ref[2 * half + 8 :, :] = jnp.zeros((8, LANES), jnp.float32)

    barrier = pltpu.get_barrier_semaphore()
    for step in range(1, bins):
        pl.semaphore_signal(
            barrier, inc=1, device_id={"bins": lax.rem(place + step, bins)}, device_id_type=mesh_ids
        )
    pl.semaphore_signal(barrier, inc=1, device_id={"fdot": mate}, device_id_type=mesh_ids)
    pl.semaphore_wait(barrier, bins)

    start = pl.multiple_of((1 - side) * (2 * half - 8), 8)
    trade = pltpu.make_async_remote_copy(
        src_ref=spec_ref.at[pl.ds(start, 2 * half + 8), :],
        dst_ref=mirror_ref.at[pl.ds(0, 2 * half + 8), :],
        send_sem=trade_send,
        recv_sem=trade_recv,
        device_id={"bins": partner},
        device_id_type=mesh_ids,
    )
    tile_copies = []
    for step in range(1, bins):
        tile_copies.append(
            pltpu.make_async_remote_copy(
                src_ref=tiles_ref.at[place],
                dst_ref=tiles_ref.at[place],
                send_sem=tile_send.at[step],
                recv_sem=tile_recv.at[step],
                device_id={"bins": lax.rem(place + step, bins)},
                device_id_type=mesh_ids,
            )
        )
    for copy in tile_copies:
        copy.start()
    trade.start()

    position = place * (block_rows * LANES) + (side * half + line) * LANES + lane
    angle = position.astype(jnp.float32) * jnp.float32(math.pi / total_bins)
    cosine = jnp.cos(angle)
    sine = jnp.sin(angle)

    for step in range(1, bins):
        source = lax.rem(place + bins - step, bins)
        pltpu.make_async_remote_copy(
            src_ref=tiles_ref.at[source],
            dst_ref=tiles_ref.at[source],
            send_sem=tile_send.at[step],
            recv_sem=tile_recv.at[step],
            device_id={"bins": lax.rem(place + step, bins)},
            device_id_type=mesh_ids,
        ).wait_recv()
    power = tiles_ref[0, :8, :]
    for other in range(1, bins):
        power = power + tiles_ref[other, :8, :]
    total = jnp.sum(jnp.sum(power, axis=0, keepdims=True), axis=1, keepdims=True)
    scaling = lax.rsqrt(total / total_bins + 1e-06)
    after = tiles_ref[lax.rem(bins - place, bins), 8:, :]

    trade.wait_recv()
    own = pl.multiple_of(side * 2 * half, 8)
    base = pl.multiple_of((1 - side) * 8, 8)
    turn = (LANES - lane[:8]) & (LANES - 1)
    flip = 7 - line[:8]
    at_last = (line == half - 1) & (side == 0)
    mirrored = []
    for part in range(2):
        here = mirror_ref[pl.ds(base + part, half, stride=2), :]
        follow = mirror_ref[pl.ds(base + part + 2, half, stride=2), :]
        follow = jnp.where(at_last, after[part : part + 1, :], follow)
        groups = []
        for first in range(half - 8, -1, -8):
            piece = jnp.take_along_axis(here[first : first + 8, :], turn, axis=1)
            piece = jnp.where(lane[:8] == 0, follow[first : first + 8, :], piece)
            groups.append(jnp.take_along_axis(piece, flip, axis=0))
        mirrored.append(jnp.concatenate(groups, axis=0))
    real_a = spec_ref[pl.ds(own, half, stride=2), :]
    imag_a = spec_ref[pl.ds(own + 1, half, stride=2), :]
    real_b, imag_b = mirrored
    even_real = 0.5 * (real_a + real_b)
    even_imag = 0.5 * (imag_a - imag_b)
    odd_real = 0.5 * (imag_a + imag_b)
    odd_imag = 0.5 * (real_b - real_a)
    out_real = even_real + cosine * odd_real + sine * odd_imag
    out_imag = even_imag + cosine * odd_imag - sine * odd_real
    mine = place * 2 + side
    out_ref[mine, 0] = (out_real * scaling).astype(jnp.bfloat16)
    out_ref[mine, 1] = (out_imag * scaling).astype(jnp.bfloat16)

    def to_bins(slot, step):
        return pltpu.make_async_remote_copy(
            src_ref=out_ref.at[slot],
            dst_ref=out_ref.at[slot],
            send_sem=part_send.at[step],
            recv_sem=part_recv.at[step],
            device_id={"bins": lax.rem(place + step, bins)},
            device_id_type=mesh_ids,
        )

    def to_mate(slot, step):
        return pltpu.make_async_remote_copy(
            src_ref=out_ref.at[slot],
            dst_ref=out_ref.at[slot],
            send_sem=mate_send.at[step],
            recv_sem=mate_recv.at[step],
            device_id={"fdot": mate},
            device_id_type=mesh_ids,
        )

    sends = [to_bins(mine, step) for step in range(1, bins)] + [to_mate(mine, 0)]
    for copy in sends:
        copy.start()
    for step in range(1, bins):
        slot = lax.rem(place + bins - step, bins) * 2 + side
        to_bins(slot, step).wait_recv()
        copy = to_mate(slot, step)
        copy.start()
        sends.append(copy)
    for step in range(bins):
        slot = lax.rem(place + bins - step, bins) * 2 + 1 - side
        to_mate(slot, step).wait_recv()
    trade.wait_send()
    for copy in tile_copies + sends:
        copy.wait_send()


def spread(spectrum):
    bins = lax.axis_size("bins")
    block_rows = spectrum.shape[1] // LANES
    half = block_rows // 2
    lines = spectrum.reshape(2, block_rows, LANES).transpose(1, 0, 2).reshape(2 * block_rows, LANES)
    vmem = pl.BlockSpec(memory_space=pltpu.VMEM)

    def kernel(*refs):
        spread_kernel(bins, *refs)

    dma = pltpu.SemaphoreType.DMA
    return pl.pallas_call(
        kernel,
        out_shape=jax.ShapeDtypeStruct((2 * bins, 2, half, LANES), jnp.bfloat16),
        in_specs=[vmem],
        out_specs=vmem,
        scratch_shapes=[
            pltpu.VMEM((2 * half + 16, LANES), jnp.float32),
            pltpu.VMEM((bins, 16, LANES), jnp.float32),
            dma, dma, dma((bins,)), dma((bins,)), dma((bins,)), dma((bins,)), dma((bins,)), dma((bins,)),
        ],
        compiler_params=pltpu.CompilerParams(collective_id=0, has_side_effects=True),
        name="spread",
    )(lines)


def search_layout(block_rows):
    spans = [(8, 0, block_rows)]
    row = block_rows
    for stride in STRIDE_TABLE:
        count = stride * block_rows // 8 + 16
        spans.append((stride, row, count))
        row += count
    return spans, row


def search_kernel(block_rows, templates, harm_ref, index_ref, bank_ref, spec_ref, out_ref,
                  lines_ref, window_ref, weight_ref, plane_ref):
    spans, _ = search_layout(block_rows)
    half = spec_ref.shape[2]
    total_rows = spec_ref.shape[0] * half
    position = lax.axis_index("bins")
    bank_rows = bank_ref.shape[0]
    lane_of = lax.broadcasted_iota(jnp.int32, (2 * templates, bank_rows), 1)
    line_of = lax.broadcasted_iota(jnp.int32, (2 * templates, bank_rows), 0)
    chosen = jnp.zeros((2 * templates, bank_rows), jnp.int32)
    for template in range(index_ref.shape[0]):
        chosen = jnp.where(line_of == template, 2 * index_ref[template], chosen)
        chosen = jnp.where(line_of == templates + template, 2 * index_ref[template] + 1, chosen)
    onehot = jnp.where(chosen == lane_of, 1.0, 0.0).astype(jnp.bfloat16)
    taps = jnp.dot(onehot, bank_ref[...], preferred_element_type=jnp.float32).astype(jnp.bfloat16)
    tap = lax.broadcasted_iota(jnp.int32, (LANES, 2 * LANES), 0)
    lane = lax.broadcasted_iota(jnp.int32, (LANES, 2 * LANES), 1)
    turn = jnp.where((tap + lane) % (2 * LANES) == 0, 1.0, 0.0).astype(jnp.bfloat16)
    turned = jnp.dot(taps, turn, preferred_element_type=jnp.float32)
    for template in range(templates):
        parts = []
        for part in range(2):
            line = part * templates + template
            row = jnp.broadcast_to(turned[line : line + 1, :], (2 * LANES, 2 * LANES))
            rolled = pltpu.roll(row, 0, 1, stride=1, stride_axis=0)
            parts.append(rolled[:, :LANES].astype(jnp.bfloat16))
        real, imag = parts
        weight_ref[template, : 2 * LANES, :LANES] = real
        weight_ref[template, : 2 * LANES, LANES:] = imag
        weight_ref[template, 2 * LANES :, :LANES] = -imag
        weight_ref[template, 2 * LANES :, LANES:] = real
    for part in range(2):
        lines_ref[part, :8, :] = jnp.zeros((8, LANES), jnp.float32)
        lines_ref[part, pl.ds(8 + total_rows, 8), :] = jnp.zeros((8, LANES), jnp.float32)

    @pl.loop(0, spec_ref.shape[0])
    def _(step):
        row = pl.multiple_of(step * half, half)
        for part in range(2):
            lines_ref[part, pl.ds(row + 8, half), :] = pltpu.roll(
                spec_ref[step, part].astype(jnp.float32), LANES // 2, 1
            )

    low_half = lax.broadcasted_iota(jnp.int32, (half, LANES), 1) < LANES // 2

    @pl.loop(0, spec_ref.shape[0])
    def _(step):
        row = pl.multiple_of(step * half, half)
        target = pl.ds(row, half)
        for part in range(2):
            before = lines_ref[part, pl.ds(row + 7, half), :]
            here = lines_ref[part, pl.ds(row + 8, half), :]
            after = lines_ref[part, pl.ds(row + 9, half), :]
            window_ref[target, 2 * part * LANES : (2 * part + 1) * LANES] = jnp.where(
                low_half, before, here
            ).astype(jnp.bfloat16)
            window_ref[target, (2 * part + 1) * LANES : (2 * part + 2) * LANES] = jnp.where(
                low_half, here, after
            ).astype(jnp.bfloat16)

    @pl.loop(0, templates)
    def _(template):
        weight = weight_ref[template]
        for stride, first, count in spans:
            start = pl.multiple_of(position * (stride * block_rows // 8), 16)
            amps = jnp.dot(
                window_ref[pl.ds(start, count), :], weight, preferred_element_type=jnp.float32
            )
            real, imag = amps[:, :LANES], amps[:, LANES:]
            plane_ref[pl.ds(first * templates + template, count, stride=templates), :] = (
                real * real + imag * imag
            )

    column = lax.broadcasted_iota(jnp.int32, (templates, LANES), 1)
    wide = 8
    bases = [
        (column * stride + harm_ref[3, number]) >> 3 for number, stride in enumerate(STRIDE_TABLE)
    ]

    @pl.loop(0, block_rows // (8 * wide))
    def _(block):
        def rows_at(line):
            row = pl.multiple_of(line * templates, templates)
            return plane_ref[pl.ds(row, templates), :]

        for unit in range(8):
            sums = [rows_at((block * wide + group) * 8 + unit) for group in range(wide)]
            for number, (stride, first, _) in enumerate(spans[1:]):
                begin = unit * stride * (LANES // 8)
                line, offset = begin // LANES, begin % LANES
                where = bases[number] + offset
                wrapped = where & (LANES - 1)
                straddles = offset + stride * (LANES // 8) >= LANES
                inside = where < LANES
                for group in range(wide):
                    source = first + (block * wide + group) * stride + line
                    picked = jnp.take_along_axis(rows_at(source), wrapped, axis=1)
                    if straddles:
                        follow = jnp.take_along_axis(rows_at(source + 1), wrapped, axis=1)
                        picked = jnp.where(inside, picked, follow)
                    sums[group] = sums[group] + picked
            for group in range(wide):
                row = pl.multiple_of(((block * wide + group) * 8 + unit) * templates, templates)
                out_ref[pl.ds(row, templates), :] = sums[group] * 0.125


def search(pieces, bank, fdot_index, harm_map, block_rows):
    own = fdot_index.shape[0]
    templates = -(-own // 8) * 8
    n_bank = bank.shape[0]
    total_rows = pieces.shape[0] * pieces.shape[2]
    _, plane_rows = search_layout(block_rows)
    vmem = pl.BlockSpec(memory_space=pltpu.VMEM)
    smem = pl.BlockSpec(memory_space=pltpu.SMEM)

    def kernel(*refs):
        search_kernel(block_rows, templates, *refs)

    out = pl.pallas_call(
        kernel,
        out_shape=jax.ShapeDtypeStruct((block_rows * templates, LANES), jnp.float32),
        in_specs=[smem, smem, vmem, vmem],
        out_specs=vmem,
        scratch_shapes=[
            pltpu.VMEM((2, total_rows + 16, LANES), jnp.float32),
            pltpu.VMEM((total_rows, 4 * LANES), jnp.bfloat16),
            pltpu.VMEM((templates, 4 * LANES, 2 * LANES), jnp.bfloat16),
            pltpu.VMEM((plane_rows * templates, LANES), jnp.float32),
        ],
        compiler_params=pltpu.CompilerParams(vmem_limit_bytes=56 * 1024 * 1024),
        name="search",
    )(harm_map[:, 0, :].T, fdot_index, bank.reshape(2 * n_bank, LANES), pieces)
    out = out.reshape(block_rows, templates, LANES).transpose(1, 0, 2)
    return out.reshape(templates, block_rows * LANES)[:own]


def body(spectrum, bank, fdot_index, harm_map):
    pieces = spread(spectrum)
    return search(pieces, bank, fdot_index, harm_map, spectrum.shape[1] // LANES)


def solution(mesh):
    placed = (P(None, ("groups", "bins")), P(), P("fdot"), P(None, "bins", None))
    return jax.shard_map(
        body, mesh=mesh, in_specs=placed, out_specs=P("fdot", ("groups", "bins")), check_vma=False
    )
```

```python
import math

import jax
import jax.numpy as jnp
from jax import lax
from jax.experimental import pallas as pl
from jax.experimental.pallas import tpu as pltpu
from jax.sharding import PartitionSpec as P

LANES = 128
STRIDE_TABLE = (4, 2, 6, 1, 3, 5, 7)


WAYS = 4


def unpack(real_a, imag_a, real_b, imag_b, position, total_bins):
    even_real = 0.5 * (real_a + real_b)
    even_imag = 0.5 * (imag_a - imag_b)
    odd_real = 0.5 * (imag_a + imag_b)
    odd_imag = 0.5 * (real_b - real_a)
    angle = position.astype(jnp.float32) * jnp.float32(math.pi / total_bins)
    cosine = jnp.cos(angle)
    sine = jnp.sin(angle)
    out_real = even_real + cosine * odd_real + sine * odd_imag
    out_imag = even_imag + cosine * odd_imag - sine * odd_real
    return out_real, out_imag


def mirror(here, follow):
    lane = lax.broadcasted_iota(jnp.int32, (8, LANES), 1)
    turn = (LANES - lane) & (LANES - 1)
    flip = 7 - lax.broadcasted_iota(jnp.int32, (8, LANES), 0)
    groups = []
    for first in range(here.shape[0] - 8, -1, -8):
        piece = jnp.take_along_axis(here[first : first + 8, :], turn, axis=1)
        piece = jnp.where(lane == 0, follow[first : first + 8, :], piece)
        groups.append(jnp.take_along_axis(piece, flip, axis=0))
    return jnp.concatenate(groups, axis=0)


def spread_kernel(bins, spec_ref, out_ref, mirror_ref, tiles_ref, trade_send, trade_recv,
                  tile_send, tile_recv, part_send, part_recv, side_send, side_recv,
                  mate_send, mate_recv):
    mesh_ids = pl.DeviceIdType.MESH
    block_rows = spec_ref.shape[0] // 2
    unit = block_rows // (2 * WAYS)
    place = lax.axis_index("bins")
    whole_member = lax.axis_index("fdot")
    member = lax.rem(whole_member, WAYS)
    mate = whole_member + 1 - 2 * lax.rem(member, 2)
    across = whole_member + 2 - 4 * (member // 2)
    mate_member = member + 1 - 2 * lax.rem(member, 2)
    across_member = member + 2 - 4 * (member // 2)
    mate_across = mate_member + 2 - 4 * (mate_member // 2)
    partner = bins - 1 - place
    total_bins = bins * block_rows * LANES
    edge = jnp.where(member == 0, 1, 0)

    power = jnp.zeros((8, LANES), jnp.float32)
    for first in range(0, 2 * block_rows, 64):
        chunk = spec_ref[first : first + 64, :]
        square = chunk * chunk
        if first == 0:
            row8 = lax.broadcasted_iota(jnp.int32, (64, LANES), 0)
            lane8 = lax.broadcasted_iota(jnp.int32, (64, LANES), 1)
            both = chunk[0:1, :] + chunk[1:2, :]
            is_first = (lane8 == 0) & (place == 0)
            square = jnp.where(is_first & (row8 == 0), both * both, square)
            square = jnp.where(is_first & (row8 == 1), 0.0, square)
        power = power + jnp.sum(square.reshape(8, 8, LANES), axis=0)
    tiles_ref[place, :8, :] = power
    tiles_ref[place, 8:, :] = spec_ref[:8, :]
    mirror_ref[2 * unit + 8 :, :] = jnp.zeros((8, LANES), jnp.float32)

    barrier = pltpu.get_barrier_semaphore()
    for step in range(1, bins):
        pl.semaphore_signal(
            barrier, inc=1, device_id={"bins": lax.rem(place + step, bins)}, device_id_type=mesh_ids
        )
    for other in (mate, across):
        pl.semaphore_signal(barrier, inc=1, device_id={"fdot": other}, device_id_type=mesh_ids)
    pl.semaphore_wait(barrier, bins + 1)

    low = 2 * unit * member
    high = block_rows - unit - low
    start = pl.multiple_of(2 * high - 8 * edge, 8)
    trade = pltpu.make_async_remote_copy(
        src_ref=spec_ref.at[pl.ds(start, 2 * unit + 8), :],
        dst_ref=mirror_ref.at[pl.ds(0, 2 * unit + 8), :],
        send_sem=trade_send,
        recv_sem=trade_recv,
        device_id={"bins": partner},
        device_id_type=mesh_ids,
    )

    def tile_copy(slot, step):
        return pltpu.make_async_remote_copy(
            src_ref=tiles_ref.at[slot],
            dst_ref=tiles_ref.at[slot],
            send_sem=tile_send.at[step],
            recv_sem=tile_recv.at[step],
            device_id={"bins": lax.rem(place + step, bins)},
            device_id_type=mesh_ids,
        )

    def piece_copy(slot, step, send, recv, device):
        return pltpu.make_async_remote_copy(
            src_ref=out_ref.at[slot],
            dst_ref=out_ref.at[slot],
            send_sem=send.at[step],
            recv_sem=recv.at[step],
            device_id=device,
            device_id_type=mesh_ids,
        )

    def to_bins(slot, step):
        device = {"bins": lax.rem(place + step, bins)}
        return piece_copy(slot, step, part_send, part_recv, device)

    def to_across(slot, step):
        return piece_copy(slot, step, side_send, side_recv, {"fdot": across})

    def to_mate(slot, step):
        return piece_copy(slot, step, mate_send, mate_recv, {"fdot": mate})

    tile_copies = [tile_copy(place, step) for step in range(bins - 1, 0, -1)]
    trade.start()
    for copy in tile_copies:
        copy.start()

    lane = lax.broadcasted_iota(jnp.int32, (unit, LANES), 1)
    line = lax.broadcasted_iota(jnp.int32, (unit, LANES), 0)
    own_position = (place * block_rows + low + line) * LANES + lane
    far_position = (partner * block_rows + high + line) * LANES + lane

    for step in range(1, bins):
        tile_copy(lax.rem(place + bins - step, bins), step).wait_recv()
    power = tiles_ref[0, :8, :]
    for other in range(1, bins):
        power = power + tiles_ref[other, :8, :]
    total = jnp.sum(jnp.sum(power, axis=0, keepdims=True), axis=1, keepdims=True)
    scaling = lax.rsqrt(total / total_bins + 1e-06)
    after = tiles_ref[lax.rem(bins - place, bins), 8:, :]
    own_row = pl.multiple_of(2 * low, 8)
    base = pl.multiple_of(8 * edge, 8)
    own = [spec_ref[pl.ds(own_row + part, unit, stride=2), :] for part in range(2)]
    own_follow = [spec_ref[pl.ds(own_row + part + 2, unit, stride=2), :] for part in range(2)]
    own_mirror = [mirror(own[part], own_follow[part]) for part in range(2)]
    at_last = (line == unit - 1) & (member == 0)

    trade.wait_recv()
    far = [mirror_ref[pl.ds(base + part, unit, stride=2), :] for part in range(2)]
    far_follow = [
        jnp.where(
            at_last,
            after[part : part + 1, :],
            mirror_ref[pl.ds(base + part + 2, unit, stride=2), :],
        )
        for part in range(2)
    ]
    far_mirror = [mirror(far[part], far_follow[part]) for part in range(2)]
    mine = place * WAYS + member
    near_out = unpack(*own, *far_mirror, own_position, total_bins)
    far_out = unpack(*far, *own_mirror, far_position, total_bins)
    for which, values in enumerate((near_out, far_out)):
        for part in range(2):
            out_ref[mine, which, part] = (values[part] * scaling).astype(jnp.bfloat16)

    sends = [to_bins(mine, step) for step in range(bins - 1, 0, -1)]
    sends += [to_across(mine, 0), to_mate(mine, 0)]
    for copy in sends:
        copy.start()

    def block_behind(step):
        return lax.rem(place + bins - step, bins) * WAYS

    def pass_bins(step):
        slot = block_behind(step) + member
        to_bins(slot, step).wait_recv()
        copies = [to_across(slot, step), to_mate(slot, step)]
        for copy in copies:
            copy.start()
        return copies

    def pass_across(step):
        slot = block_behind(step) + across_member
        to_across(slot, step).wait_recv()
        copy = to_mate(slot, bins + step)
        copy.start()
        return [copy]

    for step in range(1, bins):
        sends += pass_bins(step)
        sends += pass_across(step - 1)
    sends += pass_across(bins - 1)
    for step in range(bins):
        to_mate(block_behind(step) + mate_member, step).wait_recv()
        to_mate(block_behind(step) + mate_across, bins + step).wait_recv()
    trade.wait_send()
    for copy in tile_copies + sends:
        copy.wait_send()


def spread(spectrum):
    bins = lax.axis_size("bins")
    block_rows = spectrum.shape[1] // LANES
    unit = block_rows // (2 * WAYS)
    lines = spectrum.reshape(2, block_rows, LANES).transpose(1, 0, 2).reshape(2 * block_rows, LANES)
    vmem = pl.BlockSpec(memory_space=pltpu.VMEM)

    def kernel(*refs):
        spread_kernel(bins, *refs)

    dma = pltpu.SemaphoreType.DMA
    counts = (bins, bins, bins, bins, bins, bins, 2 * bins, 2 * bins)
    return pl.pallas_call(
        kernel,
        out_shape=jax.ShapeDtypeStruct((WAYS * bins, 2, 2, unit, LANES), jnp.bfloat16),
        in_specs=[vmem],
        out_specs=vmem,
        scratch_shapes=[
            pltpu.VMEM((2 * unit + 16, LANES), jnp.float32),
            pltpu.VMEM((bins, 16, LANES), jnp.float32),
            dma,
            dma,
            *[dma((count,)) for count in counts],
        ],
        compiler_params=pltpu.CompilerParams(collective_id=0, has_side_effects=True),
        name="spread",
    )(lines)


def search_layout(block_rows):
    spans = [(8, 0, block_rows)]
    row = block_rows
    for stride in STRIDE_TABLE:
        count = stride * block_rows // 8 + 16
        spans.append((stride, row, count))
        row += count
    return spans, row


def search_kernel(block_rows, templates, harm_ref, index_ref, bank_ref, spec_ref, out_ref,
                  lines_ref, window_ref, weight_ref, plane_ref):
    spans, _ = search_layout(block_rows)
    bins = spec_ref.shape[0] // WAYS
    unit = spec_ref.shape[3]
    half = block_rows // 2
    total_rows = bins * block_rows
    position = lax.axis_index("bins")
    bank_rows = bank_ref.shape[0]
    lane_of = lax.broadcasted_iota(jnp.int32, (2 * templates, bank_rows), 1)
    line_of = lax.broadcasted_iota(jnp.int32, (2 * templates, bank_rows), 0)
    chosen = jnp.zeros((2 * templates, bank_rows), jnp.int32)
    for template in range(index_ref.shape[0]):
        chosen = jnp.where(line_of == template, 2 * index_ref[template], chosen)
        chosen = jnp.where(line_of == templates + template, 2 * index_ref[template] + 1, chosen)
    onehot = jnp.where(chosen == lane_of, 1.0, 0.0).astype(jnp.bfloat16)
    taps = jnp.dot(onehot, bank_ref[...], preferred_element_type=jnp.float32).astype(jnp.bfloat16)
    tap = lax.broadcasted_iota(jnp.int32, (LANES, 2 * LANES), 0)
    lane = lax.broadcasted_iota(jnp.int32, (LANES, 2 * LANES), 1)
    turn = jnp.where((tap + lane) % (2 * LANES) == 0, 1.0, 0.0).astype(jnp.bfloat16)
    turned = jnp.dot(taps, turn, preferred_element_type=jnp.float32)
    for template in range(templates):
        parts = []
        for part in range(2):
            line = part * templates + template
            row = jnp.broadcast_to(turned[line : line + 1, :], (2 * LANES, 2 * LANES))
            rolled = pltpu.roll(row, 0, 1, stride=1, stride_axis=0)
            parts.append(rolled[:, :LANES].astype(jnp.bfloat16))
        real, imag = parts
        weight_ref[template, : 2 * LANES, :LANES] = real
        weight_ref[template, : 2 * LANES, LANES:] = imag
        weight_ref[template, 2 * LANES :, :LANES] = -imag
        weight_ref[template, 2 * LANES :, LANES:] = real
    for part in range(2):
        lines_ref[part, :8, :] = jnp.zeros((8, LANES), jnp.float32)
        lines_ref[part, pl.ds(8 + total_rows, 8), :] = jnp.zeros((8, LANES), jnp.float32)

    @pl.loop(0, bins)
    def _(block):
        for number in range(2 * WAYS):
            if number % 2 == 0:
                slot, which = block * WAYS + number // 2, 0
            else:
                slot, which = (bins - 1 - block) * WAYS + (2 * WAYS - 1 - number) // 2, 1
            row = pl.multiple_of(block * block_rows, block_rows) + (8 + number * unit)
            for part in range(2):
                lines_ref[part, pl.ds(row, unit), :] = pltpu.roll(
                    spec_ref[slot, which, part].astype(jnp.float32), LANES // 2, 1
                )

    low_half = lax.broadcasted_iota(jnp.int32, (half, LANES), 1) < LANES // 2

    @pl.loop(0, total_rows // half)
    def _(step):
        row = pl.multiple_of(step * half, half)
        target = pl.ds(row, half)
        for part in range(2):
            before = lines_ref[part, pl.ds(row + 7, half), :]
            here = lines_ref[part, pl.ds(row + 8, half), :]
            after = lines_ref[part, pl.ds(row + 9, half), :]
            window_ref[target, 2 * part * LANES : (2 * part + 1) * LANES] = jnp.where(
                low_half, before, here
            ).astype(jnp.bfloat16)
            window_ref[target, (2 * part + 1) * LANES : (2 * part + 2) * LANES] = jnp.where(
                low_half, here, after
            ).astype(jnp.bfloat16)

    @pl.loop(0, templates)
    def _(template):
        weight = weight_ref[template]
        for stride, first, count in spans:
            start = pl.multiple_of(position * (stride * block_rows // 8), 16)
            amps = jnp.dot(
                window_ref[pl.ds(start, count), :], weight, preferred_element_type=jnp.float32
            )
            real, imag = amps[:, :LANES], amps[:, LANES:]
            plane_ref[pl.ds(first * templates + template, count, stride=templates), :] = (
                real * real + imag * imag
            )

    column = lax.broadcasted_iota(jnp.int32, (templates, LANES), 1)
    wide = 8
    bases = [
        (column * stride + harm_ref[3, number]) >> 3 for number, stride in enumerate(STRIDE_TABLE)
    ]

    @pl.loop(0, block_rows // (8 * wide))
    def _(block):
        def rows_at(line):
            row = pl.multiple_of(line * templates, templates)
            return plane_ref[pl.ds(row, templates), :]

        for unit in range(8):
            sums = [rows_at((block * wide + group) * 8 + unit) for group in range(wide)]
            for number, (stride, first, _) in enumerate(spans[1:]):
                begin = unit * stride * (LANES // 8)
                line, offset = begin // LANES, begin % LANES
                where = bases[number] + offset
                wrapped = where & (LANES - 1)
                straddles = offset + stride * (LANES // 8) >= LANES
                inside = where < LANES
                for group in range(wide):
                    source = first + (block * wide + group) * stride + line
                    picked = jnp.take_along_axis(rows_at(source), wrapped, axis=1)
                    if straddles:
                        follow = jnp.take_along_axis(rows_at(source + 1), wrapped, axis=1)
                        picked = jnp.where(inside, picked, follow)
                    sums[group] = sums[group] + picked
            for group in range(wide):
                row = pl.multiple_of(((block * wide + group) * 8 + unit) * templates, templates)
                out_ref[pl.ds(row, templates), :] = sums[group] * 0.125


def search(pieces, bank, fdot_index, harm_map, block_rows):
    own = fdot_index.shape[0]
    templates = -(-own // 8) * 8
    n_bank = bank.shape[0]
    total_rows = pieces.shape[0] * 2 * pieces.shape[3]
    _, plane_rows = search_layout(block_rows)
    vmem = pl.BlockSpec(memory_space=pltpu.VMEM)
    smem = pl.BlockSpec(memory_space=pltpu.SMEM)

    def kernel(*refs):
        search_kernel(block_rows, templates, *refs)

    out = pl.pallas_call(
        kernel,
        out_shape=jax.ShapeDtypeStruct((block_rows * templates, LANES), jnp.float32),
        in_specs=[smem, smem, vmem, vmem],
        out_specs=vmem,
        scratch_shapes=[
            pltpu.VMEM((2, total_rows + 16, LANES), jnp.float32),
            pltpu.VMEM((total_rows, 4 * LANES), jnp.bfloat16),
            pltpu.VMEM((templates, 4 * LANES, 2 * LANES), jnp.bfloat16),
            pltpu.VMEM((plane_rows * templates, LANES), jnp.float32),
        ],
        compiler_params=pltpu.CompilerParams(vmem_limit_bytes=56 * 1024 * 1024),
        name="search",
    )(harm_map[:, 0, :].T, fdot_index, bank.reshape(2 * n_bank, LANES), pieces)
    out = out.reshape(block_rows, templates, LANES).transpose(1, 0, 2)
    return out.reshape(templates, block_rows * LANES)[:own]


def body(spectrum, bank, fdot_index, harm_map):
    pieces = spread(spectrum)
    return search(pieces, bank, fdot_index, harm_map, spectrum.shape[1] // LANES)


def solution(mesh):
    placed = (P(None, ("groups", "bins")), P(), P("fdot"), P(None, "bins", None))
    return jax.shard_map(
        body, mesh=mesh, in_specs=placed, out_specs=P("fdot", ("groups", "bins")), check_vma=False
    )
```

```python
import math

import jax
import jax.numpy as jnp
from jax import lax
from jax.experimental import pallas as pl
from jax.experimental.pallas import tpu as pltpu
from jax.sharding import PartitionSpec as P

LANES = 128
STRIDE_TABLE = (4, 2, 6, 1, 3, 5, 7)


WAYS = 2


def unpack(real_a, imag_a, real_b, imag_b, position, total_bins):
    even_real = 0.5 * (real_a + real_b)
    even_imag = 0.5 * (imag_a - imag_b)
    odd_real = 0.5 * (imag_a + imag_b)
    odd_imag = 0.5 * (real_b - real_a)
    angle = position.astype(jnp.float32) * jnp.float32(math.pi / total_bins)
    cosine = jnp.cos(angle)
    sine = jnp.sin(angle)
    out_real = even_real + cosine * odd_real + sine * odd_imag
    out_imag = even_imag + cosine * odd_imag - sine * odd_real
    return out_real, out_imag


def mirror(here, follow):
    lane = lax.broadcasted_iota(jnp.int32, (8, LANES), 1)
    turn = (LANES - lane) & (LANES - 1)
    flip = 7 - lax.broadcasted_iota(jnp.int32, (8, LANES), 0)
    groups = []
    for first in range(here.shape[0] - 8, -1, -8):
        piece = jnp.take_along_axis(here[first : first + 8, :], turn, axis=1)
        piece = jnp.where(lane == 0, follow[first : first + 8, :], piece)
        groups.append(jnp.take_along_axis(piece, flip, axis=0))
    return jnp.concatenate(groups, axis=0)


def spread_kernel(bins, spec_ref, out_ref, mirror_ref, tiles_ref, trade_send, trade_recv,
                  tile_send, tile_recv, part_send, part_recv, mate_send, mate_recv):
    mesh_ids = pl.DeviceIdType.MESH
    block_rows = spec_ref.shape[0] // 2
    unit = block_rows // (2 * WAYS)
    place = lax.axis_index("bins")
    whole_member = lax.axis_index("fdot")
    member = lax.rem(whole_member, WAYS)
    mate = whole_member + 1 - 2 * lax.rem(member, 2)
    mate_member = member + 1 - 2 * lax.rem(member, 2)
    partner = bins - 1 - place
    total_bins = bins * block_rows * LANES
    edge = jnp.where(member == 0, 1, 0)

    barrier = pltpu.get_barrier_semaphore()
    for step in range(1, bins):
        pl.semaphore_signal(
            barrier, inc=1, device_id={"bins": lax.rem(place + step, bins)}, device_id_type=mesh_ids
        )
    pl.semaphore_signal(barrier, inc=1, device_id={"fdot": mate}, device_id_type=mesh_ids)

    power = jnp.zeros((8, LANES), jnp.float32)
    for first in range(0, 2 * block_rows, 64):
        chunk = spec_ref[first : first + 64, :]
        square = chunk * chunk
        if first == 0:
            row8 = lax.broadcasted_iota(jnp.int32, (64, LANES), 0)
            lane8 = lax.broadcasted_iota(jnp.int32, (64, LANES), 1)
            both = chunk[0:1, :] + chunk[1:2, :]
            is_first = (lane8 == 0) & (place == 0)
            square = jnp.where(is_first & (row8 == 0), both * both, square)
            square = jnp.where(is_first & (row8 == 1), 0.0, square)
        power = power + jnp.sum(square.reshape(8, 8, LANES), axis=0)
    tiles_ref[place, :8, :] = power
    tiles_ref[place, 8:, :] = spec_ref[:8, :]
    mirror_ref[2 * unit + 8 :, :] = jnp.zeros((8, LANES), jnp.float32)

    pl.semaphore_wait(barrier, bins)

    low = 2 * unit * member
    high = block_rows - unit - low
    start = pl.multiple_of(2 * high - 8 * edge, 8)
    trade = pltpu.make_async_remote_copy(
        src_ref=spec_ref.at[pl.ds(start, 2 * unit + 8), :],
        dst_ref=mirror_ref.at[pl.ds(0, 2 * unit + 8), :],
        send_sem=trade_send,
        recv_sem=trade_recv,
        device_id={"bins": partner},
        device_id_type=mesh_ids,
    )

    def tile_copy(slot, step):
        return pltpu.make_async_remote_copy(
            src_ref=tiles_ref.at[slot],
            dst_ref=tiles_ref.at[slot],
            send_sem=tile_send.at[step],
            recv_sem=tile_recv.at[step],
            device_id={"bins": lax.rem(place + step, bins)},
            device_id_type=mesh_ids,
        )

    def piece_copy(slot, step, send, recv, device):
        return pltpu.make_async_remote_copy(
            src_ref=out_ref.at[slot],
            dst_ref=out_ref.at[slot],
            send_sem=send.at[step],
            recv_sem=recv.at[step],
            device_id=device,
            device_id_type=mesh_ids,
        )

    def to_bins(slot, step):
        device = {"bins": lax.rem(place + step, bins)}
        return piece_copy(slot, step, part_send, part_recv, device)

    def to_mate(slot, step):
        return piece_copy(slot, step, mate_send, mate_recv, {"fdot": mate})

    tile_copies = [tile_copy(place, step) for step in range(bins - 1, 0, -1)]
    trade.start()
    for copy in tile_copies:
        copy.start()

    lane = lax.broadcasted_iota(jnp.int32, (unit, LANES), 1)
    line = lax.broadcasted_iota(jnp.int32, (unit, LANES), 0)
    own_position = (place * block_rows + low + line) * LANES + lane
    far_position = (partner * block_rows + high + line) * LANES + lane

    for step in range(1, bins):
        tile_copy(lax.rem(place + bins - step, bins), step).wait_recv()
    power = tiles_ref[0, :8, :]
    for other in range(1, bins):
        power = power + tiles_ref[other, :8, :]
    total = jnp.sum(jnp.sum(power, axis=0, keepdims=True), axis=1, keepdims=True)
    scaling = lax.rsqrt(total / total_bins + 1e-06)
    after = tiles_ref[lax.rem(bins - place, bins), 8:, :]
    own_row = pl.multiple_of(2 * low, 8)
    base = pl.multiple_of(8 * edge, 8)
    own = [spec_ref[pl.ds(own_row + part, unit, stride=2), :] for part in range(2)]
    own_follow = [spec_ref[pl.ds(own_row + part + 2, unit, stride=2), :] for part in range(2)]
    own_mirror = [mirror(own[part], own_follow[part]) for part in range(2)]
    at_last = (line == unit - 1) & (member == 0)

    trade.wait_recv()
    far = [mirror_ref[pl.ds(base + part, unit, stride=2), :] for part in range(2)]
    far_follow = [
        jnp.where(
            at_last,
            after[part : part + 1, :],
            mirror_ref[pl.ds(base + part + 2, unit, stride=2), :],
        )
        for part in range(2)
    ]
    far_mirror = [mirror(far[part], far_follow[part]) for part in range(2)]
    mine = place * WAYS + member
    near_out = unpack(*own, *far_mirror, own_position, total_bins)
    far_out = unpack(*far, *own_mirror, far_position, total_bins)
    for which, values in enumerate((near_out, far_out)):
        for part in range(2):
            out_ref[mine, which, part] = (values[part] * scaling).astype(jnp.bfloat16)

    sends = [to_bins(mine, step) for step in range(bins - 1, 0, -1)]
    sends.append(to_mate(mine, 0))
    for copy in sends:
        copy.start()

    def block_behind(step):
        return lax.rem(place + bins - step, bins) * WAYS

    for step in range(1, bins):
        slot = block_behind(step) + member
        to_bins(slot, step).wait_recv()
        copy = to_mate(slot, step)
        copy.start()
        sends.append(copy)
    for step in range(bins):
        to_mate(block_behind(step) + mate_member, step).wait_recv()
    trade.wait_send()
    for copy in tile_copies + sends:
        copy.wait_send()


def spread(spectrum):
    bins = lax.axis_size("bins")
    block_rows = spectrum.shape[1] // LANES
    unit = block_rows // (2 * WAYS)
    lines = spectrum.reshape(2, block_rows, LANES).transpose(1, 0, 2).reshape(2 * block_rows, LANES)
    vmem = pl.BlockSpec(memory_space=pltpu.VMEM)

    def kernel(*refs):
        spread_kernel(bins, *refs)

    dma = pltpu.SemaphoreType.DMA
    return pl.pallas_call(
        kernel,
        out_shape=pltpu.VMEM((WAYS * bins, 2, 2, unit, LANES), jnp.bfloat16),
        in_specs=[vmem],
        out_specs=vmem,
        scratch_shapes=[
            pltpu.VMEM((2 * unit + 16, LANES), jnp.float32),
            pltpu.VMEM((bins, 16, LANES), jnp.float32),
            dma,
            dma,
            *[dma((bins,)) for _ in range(6)],
        ],
        compiler_params=pltpu.CompilerParams(collective_id=0, has_side_effects=True, vmem_limit_bytes=16 * 1024 * 1024
        ),
        name="spread",
    )(lines)


def search_layout(block_rows):
    spans = [(8, 0, block_rows)]
    row = block_rows
    for stride in STRIDE_TABLE:
        count = stride * block_rows // 8 + 16
        spans.append((stride, row, count))
        row += count
    return spans, row


def search_kernel(block_rows, templates, harm_ref, index_ref, bank_ref, spec_ref, out_ref,
                  lines_ref, window_ref, weight_ref, plane_ref):
    spans, _ = search_layout(block_rows)
    bins = spec_ref.shape[0] // WAYS
    unit = spec_ref.shape[3]
    half = block_rows // 2
    total_rows = bins * block_rows
    position = lax.axis_index("bins")
    bank_rows = bank_ref.shape[0]
    lane_of = lax.broadcasted_iota(jnp.int32, (2 * templates, bank_rows), 1)
    line_of = lax.broadcasted_iota(jnp.int32, (2 * templates, bank_rows), 0)
    chosen = jnp.zeros((2 * templates, bank_rows), jnp.int32)
    for template in range(index_ref.shape[0]):
        chosen = jnp.where(line_of == template, 2 * index_ref[template], chosen)
        chosen = jnp.where(line_of == templates + template, 2 * index_ref[template] + 1, chosen)
    onehot = jnp.where(chosen == lane_of, 1.0, 0.0).astype(jnp.bfloat16)
    taps = jnp.dot(onehot, bank_ref[...], preferred_element_type=jnp.float32).astype(jnp.bfloat16)
    tap = lax.broadcasted_iota(jnp.int32, (LANES, 2 * LANES), 0)
    lane = lax.broadcasted_iota(jnp.int32, (LANES, 2 * LANES), 1)
    turn = jnp.where((tap + lane) % (2 * LANES) == 0, 1.0, 0.0).astype(jnp.bfloat16)
    turned = jnp.dot(taps, turn, preferred_element_type=jnp.float32)
    for template in range(templates):
        parts = []
        for part in range(2):
            line = part * templates + template
            row = jnp.broadcast_to(turned[line : line + 1, :], (2 * LANES, 2 * LANES))
            rolled = pltpu.roll(row, 0, 1, stride=1, stride_axis=0)
            parts.append(rolled[:, :LANES].astype(jnp.bfloat16))
        real, imag = parts
        weight_ref[template, : 2 * LANES, :LANES] = real
        weight_ref[template, : 2 * LANES, LANES:] = imag
        weight_ref[template, 2 * LANES :, :LANES] = -imag
        weight_ref[template, 2 * LANES :, LANES:] = real
    for part in range(2):
        lines_ref[part, :8, :] = jnp.zeros((8, LANES), jnp.float32)
        lines_ref[part, pl.ds(8 + total_rows, 8), :] = jnp.zeros((8, LANES), jnp.float32)

    @pl.loop(0, bins)
    def _(block):
        for number in range(2 * WAYS):
            if number % 2 == 0:
                slot, which = block * WAYS + number // 2, 0
            else:
                slot, which = (bins - 1 - block) * WAYS + (2 * WAYS - 1 - number) // 2, 1
            row = pl.multiple_of(block * block_rows, block_rows) + (8 + number * unit)
            for part in range(2):
                lines_ref[part, pl.ds(row, unit), :] = pltpu.roll(
                    spec_ref[slot, which, part].astype(jnp.float32), LANES // 2, 1
                )

    low_half = lax.broadcasted_iota(jnp.int32, (half, LANES), 1) < LANES // 2

    @pl.loop(0, total_rows // half)
    def _(step):
        row = pl.multiple_of(step * half, half)
        target = pl.ds(row, half)
        for part in range(2):
            before = lines_ref[part, pl.ds(row + 7, half), :]
            here = lines_ref[part, pl.ds(row + 8, half), :]
            after = lines_ref[part, pl.ds(row + 9, half), :]
            window_ref[target, 2 * part * LANES : (2 * part + 1) * LANES] = jnp.where(
                low_half, before, here
            ).astype(jnp.bfloat16)
            window_ref[target, (2 * part + 1) * LANES : (2 * part + 2) * LANES] = jnp.where(
                low_half, here, after
            ).astype(jnp.bfloat16)

    @pl.loop(0, templates)
    def _(template):
        weight = weight_ref[template]
        for stride, first, count in spans:
            start = pl.multiple_of(position * (stride * block_rows // 8), 16)
            amps = jnp.dot(
                window_ref[pl.ds(start, count), :], weight, preferred_element_type=jnp.float32
            )
            real, imag = amps[:, :LANES], amps[:, LANES:]
            plane_ref[pl.ds(first * templates + template, count, stride=templates), :] = (
                real * real + imag * imag
            )

    column = lax.broadcasted_iota(jnp.int32, (templates, LANES), 1)
    wide = 8
    bases = [
        (column * stride + harm_ref[3, number]) >> 3 for number, stride in enumerate(STRIDE_TABLE)
    ]

    @pl.loop(0, block_rows // (8 * wide))
    def _(block):
        def rows_at(line):
            row = pl.multiple_of(line * templates, templates)
            return plane_ref[pl.ds(row, templates), :]

        for unit in range(8):
            sums = [rows_at((block * wide + group) * 8 + unit) for group in range(wide)]
            for number, (stride, first, _) in enumerate(spans[1:]):
                begin = unit * stride * (LANES // 8)
                line, offset = begin // LANES, begin % LANES
                where = bases[number] + offset
                wrapped = where & (LANES - 1)
                straddles = offset + stride * (LANES // 8) >= LANES
                inside = where < LANES
                for group in range(wide):
                    source = first + (block * wide + group) * stride + line
                    picked = jnp.take_along_axis(rows_at(source), wrapped, axis=1)
                    if straddles:
                        follow = jnp.take_along_axis(rows_at(source + 1), wrapped, axis=1)
                        picked = jnp.where(inside, picked, follow)
                    sums[group] = sums[group] + picked
            for group in range(wide):
                row = pl.multiple_of(((block * wide + group) * 8 + unit) * templates, templates)
                out_ref[pl.ds(row, templates), :] = sums[group] * 0.125


def search(pieces, bank, fdot_index, harm_map, block_rows):
    own = fdot_index.shape[0]
    templates = -(-own // 8) * 8
    n_bank = bank.shape[0]
    total_rows = pieces.shape[0] * 2 * pieces.shape[3]
    _, plane_rows = search_layout(block_rows)
    vmem = pl.BlockSpec(memory_space=pltpu.VMEM)
    smem = pl.BlockSpec(memory_space=pltpu.SMEM)

    def kernel(*refs):
        search_kernel(block_rows, templates, *refs)

    out = pl.pallas_call(
        kernel,
        out_shape=jax.ShapeDtypeStruct((block_rows * templates, LANES), jnp.float32),
        in_specs=[smem, smem, vmem, vmem],
        out_specs=vmem,
        scratch_shapes=[
            pltpu.VMEM((2, total_rows + 16, LANES), jnp.float32),
            pltpu.VMEM((total_rows, 4 * LANES), jnp.bfloat16),
            pltpu.VMEM((templates, 4 * LANES, 2 * LANES), jnp.bfloat16),
            pltpu.VMEM((plane_rows * templates, LANES), jnp.float32),
        ],
        compiler_params=pltpu.CompilerParams(vmem_limit_bytes=40 * 1024 * 1024),
        name="search",
    )(harm_map[:, 0, :].T, fdot_index, bank.reshape(2 * n_bank, LANES), pieces)
    out = out.reshape(block_rows, templates, LANES).transpose(1, 0, 2)
    return out.reshape(templates, block_rows * LANES)[:own]


def body(spectrum, bank, fdot_index, harm_map):
    pieces = spread(spectrum)
    pieces = pltpu.with_memory_space_constraint(pieces, pltpu.VMEM)
    return search(pieces, bank, fdot_index, harm_map, spectrum.shape[1] // LANES)


def solution(mesh):
    placed = (P(None, ("groups", "bins")), P(), P("fdot"), P(None, "bins", None))
    return jax.shard_map(
        body, mesh=mesh, in_specs=placed, out_specs=P("fdot", ("groups", "bins")), check_vma=False
    )
```

```python
import math

import jax
import jax.numpy as jnp
from jax import lax
from jax.experimental import pallas as pl
from jax.experimental.pallas import tpu as pltpu
from jax.sharding import PartitionSpec as P

LANES = 128
STRIDE_TABLE = (4, 2, 6, 1, 3, 5, 7)


WAYS = 2


def unpack(real_a, imag_a, real_b, imag_b, position, total_bins):
    even_real = 0.5 * (real_a + real_b)
    even_imag = 0.5 * (imag_a - imag_b)
    odd_real = 0.5 * (imag_a + imag_b)
    odd_imag = 0.5 * (real_b - real_a)
    angle = position.astype(jnp.float32) * jnp.float32(math.pi / total_bins)
    cosine = jnp.cos(angle)
    sine = jnp.sin(angle)
    out_real = even_real + cosine * odd_real + sine * odd_imag
    out_imag = even_imag + cosine * odd_imag - sine * odd_real
    return out_real, out_imag


def mirror(here, follow):
    lane = lax.broadcasted_iota(jnp.int32, (8, LANES), 1)
    turn = (LANES - lane) & (LANES - 1)
    flip = 7 - lax.broadcasted_iota(jnp.int32, (8, LANES), 0)
    groups = []
    for first in range(here.shape[0] - 8, -1, -8):
        piece = jnp.take_along_axis(here[first : first + 8, :], turn, axis=1)
        piece = jnp.where(lane == 0, follow[first : first + 8, :], piece)
        groups.append(jnp.take_along_axis(piece, flip, axis=0))
    return jnp.concatenate(groups, axis=0)


def spread_kernel(bins, spec_ref, out_ref, mirror_ref, tiles_ref, trade_send, trade_recv,
                  tile_send, tile_recv, part_send, part_recv, mate_send, mate_recv):
    mesh_ids = pl.DeviceIdType.MESH
    block_rows = spec_ref.shape[0] // 2
    unit = block_rows // (2 * WAYS)
    place = lax.axis_index("bins")
    whole_member = lax.axis_index("fdot")
    member = lax.rem(whole_member, WAYS)
    mate = whole_member + 1 - 2 * lax.rem(member, 2)
    mate_member = member + 1 - 2 * lax.rem(member, 2)
    partner = bins - 1 - place
    total_bins = bins * block_rows * LANES
    edge = jnp.where(member == 0, 1, 0)

    barrier = pltpu.get_barrier_semaphore()
    for step in range(1, bins):
        pl.semaphore_signal(
            barrier, inc=1, device_id={"bins": lax.rem(place + step, bins)}, device_id_type=mesh_ids
        )
    pl.semaphore_signal(barrier, inc=1, device_id={"fdot": mate}, device_id_type=mesh_ids)

    power = jnp.zeros((8, LANES), jnp.float32)
    for first in range(0, 2 * block_rows, 64):
        chunk = spec_ref[first : first + 64, :]
        square = chunk * chunk
        if first == 0:
            row8 = lax.broadcasted_iota(jnp.int32, (64, LANES), 0)
            lane8 = lax.broadcasted_iota(jnp.int32, (64, LANES), 1)
            both = chunk[0:1, :] + chunk[1:2, :]
            is_first = (lane8 == 0) & (place == 0)
            square = jnp.where(is_first & (row8 == 0), both * both, square)
            square = jnp.where(is_first & (row8 == 1), 0.0, square)
        power = power + jnp.sum(square.reshape(8, 8, LANES), axis=0)
    tiles_ref[place, :8, :] = power
    tiles_ref[place, 8:, :] = spec_ref[:8, :]
    mirror_ref[2 * unit + 8 :, :] = jnp.zeros((8, LANES), jnp.float32)

    pl.semaphore_wait(barrier, bins)

    low = 2 * unit * member
    high = block_rows - unit - low
    start = pl.multiple_of(2 * high - 8 * edge, 8)
    trade = pltpu.make_async_remote_copy(
        src_ref=spec_ref.at[pl.ds(start, 2 * unit + 8), :],
        dst_ref=mirror_ref.at[pl.ds(0, 2 * unit + 8), :],
        send_sem=trade_send,
        recv_sem=trade_recv,
        device_id={"bins": partner},
        device_id_type=mesh_ids,
    )

    def tile_copy(slot, step):
        return pltpu.make_async_remote_copy(
            src_ref=tiles_ref.at[slot],
            dst_ref=tiles_ref.at[slot],
            send_sem=tile_send.at[step],
            recv_sem=tile_recv.at[step],
            device_id={"bins": lax.rem(place + step, bins)},
            device_id_type=mesh_ids,
        )

    def piece_copy(slot, step, send, recv, device):
        return pltpu.make_async_remote_copy(
            src_ref=out_ref.at[slot],
            dst_ref=out_ref.at[slot],
            send_sem=send.at[step],
            recv_sem=recv.at[step],
            device_id=device,
            device_id_type=mesh_ids,
        )

    def to_bins(slot, step):
        device = {"bins": lax.rem(place + step, bins)}
        return piece_copy(slot, step, part_send, part_recv, device)

    def to_mate(slot, step):
        return piece_copy(slot, step, mate_send, mate_recv, {"fdot": mate})

    tile_copies = [tile_copy(place, step) for step in range(bins - 1, 0, -1)]
    trade.start()
    for copy in tile_copies:
        copy.start()

    lane = lax.broadcasted_iota(jnp.int32, (unit, LANES), 1)
    line = lax.broadcasted_iota(jnp.int32, (unit, LANES), 0)
    own_position = (place * block_rows + low + line) * LANES + lane
    far_position = (partner * block_rows + high + line) * LANES + lane

    for step in range(1, bins):
        tile_copy(lax.rem(place + bins - step, bins), step).wait_recv()
    power = tiles_ref[0, :8, :]
    for other in range(1, bins):
        power = power + tiles_ref[other, :8, :]
    total = jnp.sum(jnp.sum(power, axis=0, keepdims=True), axis=1, keepdims=True)
    scaling = lax.rsqrt(total / total_bins + 1e-06)
    after = tiles_ref[lax.rem(bins - place, bins), 8:, :]
    own_row = pl.multiple_of(2 * low, 8)
    base = pl.multiple_of(8 * edge, 8)
    own = [spec_ref[pl.ds(own_row + part, unit, stride=2), :] for part in range(2)]
    own_follow = [spec_ref[pl.ds(own_row + part + 2, unit, stride=2), :] for part in range(2)]
    own_mirror = [mirror(own[part], own_follow[part]) for part in range(2)]
    at_last = (line == unit - 1) & (member == 0)

    trade.wait_recv()
    far = [mirror_ref[pl.ds(base + part, unit, stride=2), :] for part in range(2)]
    far_follow = [
        jnp.where(
            at_last,
            after[part : part + 1, :],
            mirror_ref[pl.ds(base + part + 2, unit, stride=2), :],
        )
        for part in range(2)
    ]
    far_mirror = [mirror(far[part], far_follow[part]) for part in range(2)]
    mine = place * WAYS + member
    near_out = unpack(*own, *far_mirror, own_position, total_bins)
    far_out = unpack(*far, *own_mirror, far_position, total_bins)
    for which, values in enumerate((near_out, far_out)):
        for part in range(2):
            out_ref[mine, which, part] = (values[part] * scaling).astype(jnp.bfloat16)

    sends = [to_bins(mine, step) for step in range(bins - 1, 0, -1)]
    sends.append(to_mate(mine, 0))
    for copy in sends:
        copy.start()

    def block_behind(step):
        return lax.rem(place + bins - step, bins) * WAYS

    for step in range(1, bins):
        slot = block_behind(step) + member
        to_bins(slot, step).wait_recv()
        copy = to_mate(slot, step)
        copy.start()
        sends.append(copy)
    for step in range(bins):
        to_mate(block_behind(step) + mate_member, step).wait_recv()
    trade.wait_send()
    for copy in tile_copies + sends:
        copy.wait_send()


def spread(spectrum):
    bins = lax.axis_size("bins")
    block_rows = spectrum.shape[1] // LANES
    unit = block_rows // (2 * WAYS)
    lines = spectrum.reshape(2, block_rows, LANES).transpose(1, 0, 2).reshape(2 * block_rows, LANES)
    vmem = pl.BlockSpec(memory_space=pltpu.VMEM)

    def kernel(*refs):
        spread_kernel(bins, *refs)

    dma = pltpu.SemaphoreType.DMA
    return pl.pallas_call(
        kernel,
        out_shape=pltpu.VMEM((WAYS * bins, 2, 2, unit, LANES), jnp.bfloat16),
        in_specs=[vmem],
        out_specs=vmem,
        scratch_shapes=[
            pltpu.VMEM((2 * unit + 16, LANES), jnp.float32),
            pltpu.VMEM((bins, 16, LANES), jnp.float32),
            dma,
            dma,
            *[dma((bins,)) for _ in range(6)],
        ],
        compiler_params=pltpu.CompilerParams(collective_id=0, has_side_effects=True, vmem_limit_bytes=16 * 1024 * 1024
        ),
        name="spread",
    )(lines)


def search_layout(block_rows):
    spans = [(8, 0, block_rows)]
    row = block_rows
    for stride in STRIDE_TABLE:
        count = stride * block_rows // 8 + 16
        spans.append((stride, row, count))
        row += count
    return spans, row


def search_kernel(block_rows, templates, harm_ref, index_ref, bank_ref, spec_ref, out_ref,
                  lines_ref, window_ref, weight_ref, plane_ref):
    spans, _ = search_layout(block_rows)
    bins = spec_ref.shape[0] // WAYS
    unit = spec_ref.shape[3]
    half = block_rows // 2
    total_rows = bins * block_rows
    position = lax.axis_index("bins")
    bank_rows = bank_ref.shape[0]
    lane_of = lax.broadcasted_iota(jnp.int32, (2 * templates, bank_rows), 1)
    line_of = lax.broadcasted_iota(jnp.int32, (2 * templates, bank_rows), 0)
    chosen = jnp.zeros((2 * templates, bank_rows), jnp.int32)
    for template in range(index_ref.shape[0]):
        chosen = jnp.where(line_of == template, 2 * index_ref[template], chosen)
        chosen = jnp.where(line_of == templates + template, 2 * index_ref[template] + 1, chosen)
    onehot = jnp.where(chosen == lane_of, 1.0, 0.0).astype(jnp.bfloat16)
    taps = jnp.dot(onehot, bank_ref[...], preferred_element_type=jnp.float32).astype(jnp.bfloat16)
    tap = lax.broadcasted_iota(jnp.int32, (LANES, 2 * LANES), 0)
    lane = lax.broadcasted_iota(jnp.int32, (LANES, 2 * LANES), 1)
    turn = jnp.where((tap + lane) % (2 * LANES) == 0, 1.0, 0.0).astype(jnp.bfloat16)
    turned = jnp.dot(taps, turn, preferred_element_type=jnp.float32)
    for template in range(templates):
        parts = []
        for part in range(2):
            line = part * templates + template
            row = jnp.broadcast_to(turned[line : line + 1, :], (2 * LANES, 2 * LANES))
            rolled = pltpu.roll(row, 0, 1, stride=1, stride_axis=0)
            parts.append(rolled[:, :LANES].astype(jnp.bfloat16))
        real, imag = parts
        weight_ref[template, : 2 * LANES, :LANES] = real
        weight_ref[template, : 2 * LANES, LANES:] = imag
        weight_ref[template, 2 * LANES :, :LANES] = -imag
        weight_ref[template, 2 * LANES :, LANES:] = real
    for part in range(2):
        lines_ref[part, :8, :] = jnp.zeros((8, LANES), jnp.float32)
        lines_ref[part, pl.ds(8 + total_rows, 8), :] = jnp.zeros((8, LANES), jnp.float32)

    @pl.loop(0, bins)
    def _(block):
        for number in range(2 * WAYS):
            if number % 2 == 0:
                slot, which = block * WAYS + number // 2, 0
            else:
                slot, which = (bins - 1 - block) * WAYS + (2 * WAYS - 1 - number) // 2, 1
            row = pl.multiple_of(block * block_rows, block_rows) + (8 + number * unit)
            for part in range(2):
                lines_ref[part, pl.ds(row, unit), :] = pltpu.roll(
                    spec_ref[slot, which, part].astype(jnp.float32), LANES // 2, 1
                )

    low_half = lax.broadcasted_iota(jnp.int32, (half, LANES), 1) < LANES // 2

    @pl.loop(0, total_rows // half)
    def _(step):
        row = pl.multiple_of(step * half, half)
        target = pl.ds(row, half)
        for part in range(2):
            before = lines_ref[part, pl.ds(row + 7, half), :]
            here = lines_ref[part, pl.ds(row + 8, half), :]
            after = lines_ref[part, pl.ds(row + 9, half), :]
            window_ref[target, 2 * part * LANES : (2 * part + 1) * LANES] = jnp.where(
                low_half, before, here
            ).astype(jnp.bfloat16)
            window_ref[target, (2 * part + 1) * LANES : (2 * part + 2) * LANES] = jnp.where(
                low_half, here, after
            ).astype(jnp.bfloat16)

    @pl.loop(0, templates, unroll=2)
    def _(template):
        weight = weight_ref[template]
        for stride, first, count in spans:
            start = pl.multiple_of(position * (stride * block_rows // 8), 16)
            amps = jnp.dot(
                window_ref[pl.ds(start, count), :], weight, preferred_element_type=jnp.float32
            )
            real, imag = amps[:, :LANES], amps[:, LANES:]
            plane_ref[pl.ds(first * templates + template, count, stride=templates), :] = (
                real * real + imag * imag
            )

    column = lax.broadcasted_iota(jnp.int32, (templates, LANES), 1)
    wide = 16
    bases = [
        (column * stride + harm_ref[3, number]) >> 3 for number, stride in enumerate(STRIDE_TABLE)
    ]

    @pl.loop(0, block_rows // (8 * wide))
    def _(block):
        def rows_at(line):
            row = pl.multiple_of(line * templates, templates)
            return plane_ref[pl.ds(row, templates), :]

        for unit in range(8):
            sums = [rows_at((block * wide + group) * 8 + unit) for group in range(wide)]
            for number, (stride, first, _) in enumerate(spans[1:]):
                begin = unit * stride * (LANES // 8)
                line, offset = begin // LANES, begin % LANES
                where = bases[number] + offset
                wrapped = where & (LANES - 1)
                straddles = offset + stride * (LANES // 8) >= LANES
                inside = where < LANES
                for group in range(wide):
                    source = first + (block * wide + group) * stride + line
                    picked = jnp.take_along_axis(rows_at(source), wrapped, axis=1)
                    if straddles:
                        follow = jnp.take_along_axis(rows_at(source + 1), wrapped, axis=1)
                        picked = jnp.where(inside, picked, follow)
                    sums[group] = sums[group] + picked
            for group in range(wide):
                row = pl.multiple_of(((block * wide + group) * 8 + unit) * templates, templates)
                out_ref[pl.ds(row, templates), :] = sums[group] * 0.125


def search(pieces, bank, fdot_index, harm_map, block_rows):
    own = fdot_index.shape[0]
    templates = -(-own // 8) * 8
    n_bank = bank.shape[0]
    total_rows = pieces.shape[0] * 2 * pieces.shape[3]
    _, plane_rows = search_layout(block_rows)
    vmem = pl.BlockSpec(memory_space=pltpu.VMEM)
    smem = pl.BlockSpec(memory_space=pltpu.SMEM)

    def kernel(*refs):
        search_kernel(block_rows, templates, *refs)

    out = pl.pallas_call(
        kernel,
        out_shape=jax.ShapeDtypeStruct((block_rows * templates, LANES), jnp.float32),
        in_specs=[smem, smem, vmem, vmem],
        out_specs=vmem,
        scratch_shapes=[
            pltpu.VMEM((2, total_rows + 16, LANES), jnp.float32),
            pltpu.VMEM((total_rows, 4 * LANES), jnp.bfloat16),
            pltpu.VMEM((templates, 4 * LANES, 2 * LANES), jnp.bfloat16),
            pltpu.VMEM((plane_rows * templates, LANES), jnp.float32),
        ],
        compiler_params=pltpu.CompilerParams(vmem_limit_bytes=40 * 1024 * 1024),
        name="search",
    )(harm_map[:, 0, :].T, fdot_index, bank.reshape(2 * n_bank, LANES), pieces)
    out = out.reshape(block_rows, templates, LANES).transpose(1, 0, 2)
    return out.reshape(templates, block_rows * LANES)[:own]


def body(spectrum, bank, fdot_index, harm_map):
    pieces = spread(spectrum)
    pieces = pltpu.with_memory_space_constraint(pieces, pltpu.VMEM)
    return search(pieces, bank, fdot_index, harm_map, spectrum.shape[1] // LANES)


def solution(mesh):
    placed = (P(None, ("groups", "bins")), P(), P("fdot"), P(None, "bins", None))
    return jax.shard_map(
        body, mesh=mesh, in_specs=placed, out_specs=P("fdot", ("groups", "bins")), check_vma=False
    )
```
